32 devices in a mesh: dp: 4 (over y, core), item: 8 (over z, x).
Axes of the slice: x: 2, y: 2, z: 4, core: 2. Of those that a mesh axis runs over, the one named last changes fastest.
Arguments:
- query: bfloat16 [32, 256], P(('dp', 'item')), may hold values from -40 to 40
- item_table: bfloat16 [65536, 256], P(('dp', 'item')), may hold values from -2.5 to 2.5
- context_features: bfloat16 [32, 512], P(('dp', 'item')), may hold values from -6 to 6
- candidates: int32 [32, 1024], P(('dp', 'item')), may hold values from 0 to 65535, as said below
- lengths: int32 [32], P(('dp', 'item')), may hold values from 128 to 1024, as said below
- logged_slot: int32 [32], P(('dp', 'item')), may hold values from 0 to 1023, as said below
- logging_prop: int32 [32], P(('dp', 'item')), may hold values from 256 to 4095
- w_first: bfloat16 [768, 512], replicated, may hold values from -0.21875 to 0.21875
- w_second: bfloat16 [512, 512], replicated, may hold values from -0.25 to 0.25
- w_score: bfloat16 [512], replicated, may hold values from -0.5 to 0.5
Outputs:
- section_logp: float32 [32, 1024], P(('dp', 'item'))
- log_weight: float32 [32], P(('dp', 'item'))
The draws below stay inside these ranges and needn't reach their ends.
Inputs may be any that keep to these rules, and one draw needn't show every extreme that they name: `candidates`: item ids. Among the 1024 candidate slots held by one device (its single context), at most 48 name items of any one block of 2048 consecutive ids, and for every device some block is named exactly 48 times. `lengths`: some context's list has 1024 live slots and some context's list has 128. `logged_slot`: below the context's length; the context with the longest list logs its last slot.
All inputs are finite; a program needn't handle non-finite values.
Results may differ from the reference program's by a relative error of at most 0.0003.
Values may be sent and summed in bfloat16 or wider, within the bound.
A program may use at most 64 MiB of HBM per device.

```python
import math
import jax
import jax.numpy as jnp
from jax import lax

D = 256
CF = 512
H = 512
ITEM_DEV = 2048
CTX_DEV = 1
CAND_MAX = 1024
MIN_LEN = 128
CTX = 32
ITEMS = 65536
CAP = 48
DEVICES = 32


def table_row(base_key, index):
    row_key = jax.random.fold_in(base_key, index)
    raw = jax.random.truncated_normal(row_key, -6.0, 6.0, (D,), jnp.float32)
    level = jax.random.uniform(jax.random.fold_in(row_key, 7), (), jnp.float32, 0.0, 1.0)
    spread = jnp.exp(level * jnp.log(jnp.float32(3.0))) * 2.0 / jnp.sqrt(jnp.float32(D))
    return jnp.clip(raw * spread, -2.5, 2.5)


def draw_item_table(key, part):
    base_key = jax.random.fold_in(key, 101)
    indices = jnp.arange(ITEMS, dtype=jnp.int32)
    rows = jax.vmap(lambda index: table_row(base_key, index))(indices)
    return rows.astype(jnp.bfloat16)


def draw_query(key, part):
    entries = jax.random.truncated_normal(jax.random.fold_in(key, 202), -6.0, 6.0, (CTX, D), jnp.float32)
    return entries.astype(jnp.bfloat16)


def draw_candidates(key, part):
    block_count = CTX // CTX_DEV
    slot_count = CTX_DEV * CAND_MAX

    def one_block(block_key):
        keys = jax.random.split(block_key, 4)
        leader = jax.random.randint(keys[0], (), 0, block_count)
        others = CAP + jax.random.permutation(keys[1], block_count * CAP - CAP)[:slot_count - CAP]
        picked = jnp.concatenate([jnp.arange(CAP, dtype=jnp.int32), others.astype(jnp.int32)])
        holder = (leader + picked // CAP) % block_count
        holder = holder[jax.random.permutation(keys[2], slot_count)]
        inside = jax.random.randint(keys[3], (slot_count,), 0, ITEM_DEV)
        return (holder * ITEM_DEV + inside).reshape(CTX_DEV, CAND_MAX)
    keys = jax.random.split(jax.random.fold_in(key, 303), block_count)
    return jax.vmap(one_block)(keys).reshape(CTX, CAND_MAX).astype(jnp.int32)


def longest_index(key):
    keys = jax.random.split(jax.random.fold_in(key, 404), 2)
    return jax.random.randint(keys[1], (), 0, CTX)


def list_lengths(key):
    keys = jax.random.split(jax.random.fold_in(key, 404), 1)
    drawn = jax.random.randint(keys[0], (CTX,), MIN_LEN, CAND_MAX + 1)
    longest = longest_index(key)
    shortest = (longest + 1) % CTX
    drawn = drawn.at[shortest].set(MIN_LEN)
    return drawn.at[longest].set(CAND_MAX).astype(jnp.int32)


def draw_lengths(key, part):
    return list_lengths(key)


def draw_logged_slot(key, part):
    list_len = list_lengths(key)
    drawn = jax.random.randint(jax.random.fold_in(key, 505), (CTX,), 0, 1 << 20)
    slots = drawn % list_len
    longest = longest_index(key)
    shortest = (longest + 1) % CTX
    slots = slots.at[shortest].set(0)
    slots = slots.at[longest].set(CAND_MAX - 1)
    return slots.astype(jnp.int32)


def touch_ends(result, own_key, smallest, largest):
    extent = result.shape
    spot = [jax.random.randint(jax.random.fold_in(own_key, axis), (), 0, extent[axis]) for axis in range(len(extent))]
    result = result.at[tuple(spot)].set(smallest)
    longest = extent.index(max(extent))
    spot[longest] = (spot[longest] + 1) % extent[longest]
    return result.at[tuple(spot)].set(largest)


def shard_levels(rng, shape, cuts, low, high):
    level, own = 1.0, jax.random.fold_in(rng, 6)
    for position, blocks in cuts:
        steps = jnp.exp(jax.random.uniform(jax.random.fold_in(own, position), (blocks,), jnp.float32, low / len(cuts), high / len(cuts)))
        level = level * jnp.repeat(steps, shape[position] // blocks).reshape([-1 if axis == position else 1 for axis in range(len(shape))])
    return level


def centred(stream_key, shape, deviation, bound, pieces=(), kind=jnp.bfloat16):
    values = jax.random.normal(stream_key, shape, jnp.float32) * deviation
    if len(pieces) > 0:
        values = shard_levels(stream_key, shape, pieces, -0.22, 0.18) * values
    return jnp.clip(values, min=-bound, max=bound).astype(kind)


def setup_inputs(seed: int = 0) -> dict:
    streams_of = jax.random.split(jax.random.key(seed), 11)
    query = draw_query(jax.random.fold_in(streams_of[10], 71), 0)
    item_table = draw_item_table(jax.random.fold_in(streams_of[10], 71), 0)
    context_features = centred(streams_of[2], (CTX, CF), 1.0, 6.0, ((0, 32),))
    candidates = draw_candidates(jax.random.fold_in(streams_of[10], 71), 0)
    lengths = draw_lengths(jax.random.fold_in(streams_of[10], 71), 0)
    logged_slot = draw_logged_slot(jax.random.fold_in(streams_of[10], 71), 0)
    logging_prop = touch_ends(jax.random.randint(streams_of[6], (CTX,), 256, 4096), jax.random.fold_in(streams_of[6], 1), 256, 4095).astype(jnp.int32)
    w_first = centred(streams_of[7], (CF + D, H), (CF + D) ** -0.5, 0.21875)
    w_second = centred(streams_of[8], (H, H), H ** -0.5, 0.25)
    w_score = centred(streams_of[9], (H,), 128 ** -0.5, 0.5)
    return {"query": query, "item_table": item_table, "context_features": context_features, "candidates": candidates, "lengths": lengths, "logged_slot": logged_slot, "logging_prop": logging_prop, "w_first": w_first, "w_second": w_second, "w_score": w_score}


def reference(query, item_table, context_features, candidates, lengths, logged_slot, logging_prop, w_first, w_second, w_score):
    slabs = item_table.reshape(DEVICES, ITEM_DEV, D)

    def sweep(running, slab_rows):
        running_max, running_sum = running
        logits = jnp.dot(query, slab_rows.T, preferred_element_type=jnp.float32)
        new_max = jnp.maximum(running_max, jnp.max(logits, axis=1))
        new_sum = running_sum * jnp.exp(running_max - new_max) + jnp.sum(jnp.exp(logits - new_max[:, None]), axis=1)
        return (new_max, new_sum), None

    initial = (jnp.full((CTX,), -1e30, jnp.float32), jnp.zeros((CTX,), jnp.float32))
    (running_max, running_sum), unused_out = lax.scan(sweep, initial, slabs)
    log_norm = running_max + jnp.log(running_sum)
    positions = jnp.arange(CAND_MAX, dtype=jnp.int32)

    def per_context(packed):
        query_row, feature_row, item_ids, list_length, norm_value, logged_index, propensity = packed
        cand_rows = item_table[item_ids]
        gen_logit = jnp.dot(cand_rows, query_row, preferred_element_type=jnp.float32)
        context_part = jnp.dot(feature_row[None, :], w_first[:CF], preferred_element_type=jnp.float32)
        item_part = jnp.dot(cand_rows, w_first[CF:], preferred_element_type=jnp.float32)
        hidden = jax.nn.silu(item_part + context_part).astype(jnp.bfloat16)
        second = jax.nn.silu(jnp.dot(hidden, w_second, preferred_element_type=jnp.float32)).astype(jnp.bfloat16)
        score = jnp.dot(second, w_score, preferred_element_type=jnp.float32)
        live_slots = positions < list_length
        masked = jnp.where(live_slots, score, jnp.float32(-1e30))
        rank_peak = jnp.max(masked)
        rank_norm = rank_peak + jnp.log(jnp.sum(jnp.where(live_slots, jnp.exp(masked - rank_peak), jnp.float32(0.0))))
        section = jnp.where(live_slots, score - rank_norm + gen_logit - norm_value + math.log(ITEMS), jnp.float32(0.0))
        chosen = jnp.sum(jnp.where(positions == logged_index, section, jnp.float32(0.0)))
        weight = chosen + jnp.log(list_length.astype(jnp.float32)) - jnp.log(propensity.astype(jnp.float32) / 1024.0)
        return section, weight

    section_logp, log_weight = lax.map(per_context, (query, context_features, candidates, lengths, log_norm, logged_slot, logging_prop))
    return section_logp, log_weight
```

```python
import functools
import math

import jax
import jax.numpy as jnp
from jax import lax
from jax.experimental import pallas as pl
from jax.experimental.pallas import tpu as pltpu
from jax.sharding import PartitionSpec as P

F32 = jnp.float32
BF16 = jnp.bfloat16
LANES = 128
NT = (((1,), (1,)), ((), ()))
NN = (((1,), (0,)), ((), ()))
TN = (((0,), (0,)), ((), ()))


def round_up(value, step):
    return (value + step - 1) // step * step


def dot(left, right, dims):
    return lax.dot_general(left, right, dims, preferred_element_type=F32)


def silu(v):
    half = v * 0.5
    return half + half * jnp.tanh(half)


def kernel(
    dp_size,
    item_size,
    groups,
    cap,
    query_hbm,
    feature_hbm,
    cand_hbm,
    length_hbm,
    slot_hbm,
    prop_hbm,
    table_hbm,
    first_hbm,
    second_hbm,
    score_hbm,
    section_ref,
    weight_ref,
    query_ref,
    feature_ref,
    cand_ref,
    length_ref,
    slot_ref,
    prop_ref,
    score_ref,
    table,
    first,
    second_w,
    send1,
    recv1,
    send2,
    recv2,
    load_sem,
    send_sem,
    arrive_sem,
    return_sem,
    own_sem,
    items,
    found,
    wanted_v,
    wanted_at,
    index_sem,
):
    n = dp_size * item_size
    item_rows, width = table.shape
    slots = cand_ref.shape[1]
    feature_width = feature_ref.shape[1]
    hidden_width = first.shape[1]
    gen_at = round_up(cap, 8)
    max_at = 2 * gen_at
    dp_me, item_me = lax.axis_index("dp"), lax.axis_index("item")
    me = dp_me * item_size + item_me
    run = item_size // groups
    members = dp_size * run
    run_me = lax.div(item_me, run)
    member_me = dp_me * run + lax.rem(item_me, run)

    def device(offset, member):
        dp = lax.div(member, run)
        item = lax.rem(run_me + offset, groups) * run + lax.rem(member, run)
        return dp * item_size + item, {"dp": dp, "item": item}

    def each_peer(offset, act):
        @pl.loop(1 if offset == 0 else 0, members)
        def visit(j):
            member = lax.rem(member_me + j, members)
            peer, where = device(offset, member)
            act(member, peer, where)

    barrier = pltpu.get_barrier_semaphore()

    def greet(member, peer, where):
        pl.semaphore_signal(barrier, inc=1, device_id=where, device_id_type=pl.DeviceIdType.MESH)

    far_first = sorted(range(groups), key=lambda g: -min(g, groups - g))
    for offset in far_first:
        each_peer(offset, greet)

    loads = [
        pltpu.make_async_copy(source, target, load_sem.at[i])
        for i, (source, target) in enumerate(
            [
                (cand_hbm, cand_ref),
                (query_hbm, query_ref),
                (feature_hbm, feature_ref),
                (first_hbm, first),
                (table_hbm, table),
                (second_hbm, second_w),
                (score_hbm, score_ref),
                (length_hbm, length_ref),
                (slot_hbm, slot_ref),
                (prop_hbm, prop_ref),
            ]
        )
    ]
    for load in loads:
        load.start()
    loads[0].wait()

    ids = cand_ref[...]
    holder = lax.div(ids, item_rows)
    local = ids - holder * item_rows
    high = lax.div(local, LANES).astype(F32)
    low = lax.rem(local, LANES).astype(F32)
    held = (lax.broadcasted_iota(jnp.int32, (n, slots), 0) == holder).astype(F32)
    blocks = slots // LANES
    stacked = jnp.concatenate(
        [held[:, b * LANES : (b + 1) * LANES] for b in range(blocks)], axis=0
    ).astype(BF16)
    before = (
        lax.broadcasted_iota(jnp.int32, (LANES, LANES), 0)
        < lax.broadcasted_iota(jnp.int32, (LANES, LANES), 1)
    ).astype(F32)
    counter = jnp.concatenate([before, jnp.ones((LANES, LANES), F32)], axis=1).astype(BF16)
    counts = dot(stacked, counter, NN)
    total = jnp.zeros((n, LANES), F32)
    rank_parts = []
    for b in range(blocks):
        here = counts[b * n : (b + 1) * n]
        place = here[:, :LANES] + total
        rank_parts.append(
            jnp.sum(held[:, b * LANES : (b + 1) * LANES] * place, axis=0, keepdims=True)
        )
        total = total + here[:, LANES:]
    rank = jnp.concatenate(rank_parts, axis=1)
    at_rank = (
        lax.broadcasted_iota(jnp.int32, (LANES, slots), 0).astype(F32) == rank
    ).astype(F32)
    parts = jnp.concatenate([held * high, held * low], axis=0).astype(BF16)
    asked = dot(parts, at_rank.astype(BF16), NT)
    asked = asked[:n] * float(LANES) + asked[n:]

    for load in loads[1:4]:
        load.wait()
    context_part = dot(feature_ref[...], first[:feature_width, :], NN)
    send1[:, 0, :width] = jnp.broadcast_to(query_ref[...].astype(F32), (n, width))
    send1[:, 0, width : width + hidden_width] = jnp.broadcast_to(context_part, (n, hidden_width))
    send1[:, 0, width + hidden_width :] = asked

    pl.semaphore_wait(barrier, n - 1)

    def ask(offset):
        seen = (groups - offset) % groups

        def act(member, peer, where):
            pltpu.make_async_remote_copy(
                src_ref=send1.at[pl.ds(peer, 1)],
                dst_ref=recv1.at[pl.ds(seen * members + member_me, 1)],
                send_sem=send_sem.at[0],
                recv_sem=arrive_sem.at[seen],
                device_id=where,
                device_id_type=pl.DeviceIdType.MESH,
            ).start()

        each_peer(offset, act)

    def give_back(offset):
        def act(member, peer, where):
            pltpu.make_async_remote_copy(
                src_ref=send2.at[pl.ds(offset * members + member, 1)],
                dst_ref=recv2.at[pl.ds(me, 1)],
                send_sem=send_sem.at[1],
                recv_sem=return_sem,
                device_id=where,
                device_id_type=pl.DeviceIdType.MESH,
            ).start()

        each_peer(offset, act)

    def wait_rows(buffer, count, semaphore):
        rows = buffer.at[pl.ds(0, count)]
        pltpu.make_async_copy(rows, rows, semaphore).wait()

    own_ask = pltpu.make_async_copy(
        send1.at[pl.ds(me, 1)], recv1.at[pl.ds(member_me, 1)], own_sem.at[0]
    )
    own_ask.start()
    for offset in far_first:
        ask(offset)
    for load in loads[4:]:
        load.wait()
    own_ask.wait()

    lane = lax.broadcasted_iota(jnp.int32, (members, LANES), 1)
    score_rows = jnp.broadcast_to(score_ref[...].reshape(1, hidden_width), (LANES, hidden_width))
    hidden_tiles = hidden_width // LANES
    tall = items.shape[1]
    flat = items.reshape(item_rows * tall, LANES)
    step = math.gcd(256, item_rows)

    @pl.loop(0, item_rows // step)
    def project(i):
        part = pl.ds(pl.multiple_of(i * step, step), step)
        block = table[part]
        projected = dot(block, first[feature_width:, :], NN)
        base = pl.multiple_of(i * (step * tall), step * tall)

        def put(j, value):
            flat[pl.ds(base + j, step, stride=tall), :] = value

        for j in range(hidden_tiles):
            put(j, projected[:, j * LANES : (j + 1) * LANES])
        for j in range(width // LANES):
            put(hidden_tiles + j, block[:, j * LANES : (j + 1) * LANES].astype(F32))

    def to_scalar(group):
        rows_here = pl.ds(group * members, members)
        return pltpu.make_async_copy(
            wanted_v.at[rows_here], wanted_at.at[rows_here], index_sem.at[group]
        )

    def rank_group(group):
        rows_here = pl.ds(group * members, members)
        query = recv1[rows_here, 0, :width]
        context = recv1[rows_here, 0, width : width + hidden_width]
        to_scalar(group).wait()
        for r in range(cap):
            for c in range(members):
                at = wanted_at[group * members + c, 0, r]
                place = (group * cap + r) * members + c
                found[pl.ds(place * tall, tall)] = items[at]
        count = cap * members

        def found_tile(j):
            return found[pl.ds(group * count * tall + j, count, stride=tall), :]

        item_part = jnp.concatenate([found_tile(j) for j in range(hidden_tiles)], axis=1)
        rows = jnp.concatenate(
            [found_tile(hidden_tiles + j) for j in range(width // LANES)], axis=1
        )
        hidden = silu(item_part + jnp.concatenate([context] * cap, axis=0)).astype(BF16)
        second = silu(dot(hidden, second_w[...], NN)).astype(BF16)
        score = dot(second, score_rows, NT)
        result = jnp.zeros((members, LANES), F32)
        for r in range(cap):
            mine = slice(r * members, (r + 1) * members)
            gen = jnp.sum(rows[mine] * query, axis=1, keepdims=True)
            result = jnp.where(lane == r, score[mine], result)
            result = jnp.where(lane == gen_at + r, gen, result)
        return result

    def normalizers(group):
        rows_here = pl.ds(group * members, members)
        logits = dot(recv1[rows_here, 0, :width].astype(BF16), table[...], NT)
        local_max = jnp.max(logits, axis=1, keepdims=True)
        local_sum = jnp.sum(jnp.exp(logits - local_max), axis=1, keepdims=True)
        return local_max, local_sum

    order = sorted(range(groups), key=lambda g: min(g, groups - g))
    for group in order:
        rows_here = pl.ds(group * members, members)
        wait_rows(recv1, members - 1 if group == 0 else members, arrive_sem.at[group])
        asked_here = recv1[rows_here, :, width + hidden_width :].astype(jnp.int32)
        wanted_v[rows_here] = jnp.clip(asked_here, 0, item_rows - 1)
        to_scalar(group).start()
        local_max, local_sum = normalizers(group)
        result = rank_group(group)
        result = jnp.where(lane == max_at, local_max, result)
        result = jnp.where(lane == max_at + 1, local_sum, result)
        send2[rows_here, 0, :] = result
        give_back(group)
        if group == 0:
            own_back = pltpu.make_async_copy(
                send2.at[pl.ds(member_me, 1)], recv2.at[pl.ds(me, 1)], own_sem.at[1]
            )
            own_back.start()
    own_back.wait()
    wait_rows(send1, n - 1, send_sem.at[0])
    wait_rows(recv2, n - 1, return_sem)

    back = recv2[:, 0, :]
    top = back.astype(BF16)
    rest = back - top.astype(F32)
    middle = rest.astype(BF16)
    bottom = (rest - middle.astype(F32)).astype(BF16)
    pieces = jnp.concatenate([top.astype(F32), middle.astype(F32), bottom.astype(F32)], axis=0)
    held_bf = held.astype(BF16)
    spread = dot(
        pieces.astype(BF16).T, jnp.concatenate([held_bf, held_bf, held_bf], axis=0), NN
    )
    score = jnp.sum(at_rank[:gen_at] * spread[:gen_at], axis=0, keepdims=True)
    gen = jnp.sum(at_rank[:gen_at] * spread[gen_at : 2 * gen_at], axis=0, keepdims=True)

    maxima = back[:, max_at : max_at + 1]
    sums = back[:, max_at + 1 : max_at + 2]
    peak = jnp.max(maxima, axis=0, keepdims=True)
    log_norm = peak + jnp.log(jnp.sum(sums * jnp.exp(maxima - peak), axis=0, keepdims=True))

    length = length_ref[0]
    position = lax.broadcasted_iota(jnp.int32, (1, slots), 1)
    live = position < length
    masked = jnp.where(live, score, -1e30)
    rank_peak = jnp.max(masked, axis=1, keepdims=True)
    rank_norm = rank_peak + jnp.log(
        jnp.sum(jnp.where(live, jnp.exp(masked - rank_peak), 0.0), axis=1, keepdims=True)
    )
    section = jnp.where(
        live, score - rank_norm + gen - log_norm + math.log(item_rows * n), 0.0
    )
    chosen = jnp.sum(jnp.where(position == slot_ref[0], section, 0.0), axis=1, keepdims=True)
    count = jnp.full((1, 1), length, jnp.int32).astype(F32)
    prop = jnp.full((1, 1), prop_ref[0], jnp.int32).astype(F32) / 1024.0
    section_ref[...] = section
    weight_ref[...] = chosen + jnp.log(count) - jnp.log(prop)
    wait_rows(send2, n - 1, send_sem.at[1])


def solution(mesh):
    dp_size, item_size = mesh.shape["dp"], mesh.shape["item"]
    n = dp_size * item_size

    def body(
        query,
        item_table,
        context_features,
        candidates,
        lengths,
        logged_slot,
        logging_prop,
        w_first,
        w_second,
        w_score,
    ):
        slots = candidates.shape[1]
        cap = max(2, 3 * slots // (2 * n))
        width = query.shape[1]
        hidden_width = w_first.shape[1]
        message = width + hidden_width + LANES
        tall = round_up((width + hidden_width) // LANES, 8)
        vmem = pl.BlockSpec(memory_space=pltpu.VMEM)
        groups = math.gcd(4, item_size)
        section, weight = pl.pallas_call(
            functools.partial(kernel, dp_size, item_size, groups, cap),
            out_shape=(
                pltpu.VMEM((1, slots), F32),
                pltpu.VMEM((1, 1), F32),
            ),
            in_specs=[pl.BlockSpec(memory_space=pltpu.HBM)] * 10,
            out_specs=(vmem, vmem),
            scratch_shapes=[
                pltpu.VMEM(query.shape, BF16),
                pltpu.VMEM(context_features.shape, BF16),
                pltpu.VMEM(candidates.shape, jnp.int32),
                pltpu.SMEM((1,), jnp.int32),
                pltpu.SMEM((1,), jnp.int32),
                pltpu.SMEM((1,), jnp.int32),
                pltpu.VMEM(w_score.shape, BF16),
                pltpu.VMEM(item_table.shape, BF16),
                pltpu.VMEM(w_first.shape, BF16),
                pltpu.VMEM(w_second.shape, BF16),
                pltpu.VMEM((n, 1, message), F32),
                pltpu.VMEM((n, 1, message), F32),
                pltpu.VMEM((n, 1, LANES), F32),
                pltpu.VMEM((n, 1, LANES), F32),
                pltpu.SemaphoreType.DMA((10,)),
                pltpu.SemaphoreType.DMA((2,)),
                pltpu.SemaphoreType.DMA((groups,)),
                pltpu.SemaphoreType.DMA,
                pltpu.SemaphoreType.DMA((2,)),
                pltpu.VMEM((item_table.shape[0], tall, LANES), F32),
                pltpu.VMEM((n * cap * tall + tall, LANES), F32),
                pltpu.VMEM((n, 1, LANES), jnp.int32),
                pltpu.SMEM((n, 1, LANES), jnp.int32),
                pltpu.SemaphoreType.DMA((groups,)),
            ],
            compiler_params=pltpu.CompilerParams(collective_id=0, has_side_effects=True),
            name="propensity",
        )(
            query,
            context_features,
            candidates,
            lengths,
            logged_slot,
            logging_prop,
            item_table,
            w_first,
            w_second,
            w_score,
        )
        return section, weight.reshape(-1)

    split = P(("dp", "item"))
    rows = P(("dp", "item"), None)
    return jax.shard_map(
        body,
        mesh=mesh,
        in_specs=(rows, rows, rows, rows, split, split, split, P(), P(), P()),
        out_specs=(rows, split),
        check_vma=False,
    )
```

```python
import functools
import math

import jax
import jax.numpy as jnp
from jax import lax
from jax.experimental import pallas as pl
from jax.experimental.pallas import tpu as pltpu
from jax.sharding import PartitionSpec as P

F32 = jnp.float32
BF16 = jnp.bfloat16
LANES = 128
NT = (((1,), (1,)), ((), ()))
NN = (((1,), (0,)), ((), ()))
TN = (((0,), (0,)), ((), ()))


def round_up(value, step):
    return (value + step - 1) // step * step


def dot(left, right, dims):
    return lax.dot_general(left, right, dims, preferred_element_type=F32)


def silu(v):
    half = v * 0.5
    return half + half * jnp.tanh(half)


def kernel(
    dp_size,
    item_size,
    groups,
    cap,
    query_hbm,
    feature_hbm,
    cand_hbm,
    length_hbm,
    slot_hbm,
    prop_hbm,
    table_hbm,
    first_hbm,
    second_hbm,
    score_hbm,
    section_ref,
    weight_ref,
    query_ref,
    feature_ref,
    cand_ref,
    length_ref,
    slot_ref,
    prop_ref,
    score_ref,
    table,
    first,
    second_w,
    send_ids,
    send1,
    recv1,
    send2,
    recv2,
    load_sem,
    send_sem,
    arrive_sem,
    index_sem,
    return_sem,
    own_sem,
    items,
    found,
    wanted,
):
    n = dp_size * item_size
    item_rows, width = table.shape
    slots = cand_ref.shape[1]
    feature_width = feature_ref.shape[1]
    hidden_width = first.shape[1]
    gen_at = round_up(cap, 8)
    max_at = 2 * gen_at
    dp_me, item_me = lax.axis_index("dp"), lax.axis_index("item")
    me = dp_me * item_size + item_me
    run = item_size // groups
    members = dp_size * run
    run_me = lax.div(item_me, run)
    member_me = dp_me * run + lax.rem(item_me, run)

    def device(offset, member):
        dp = lax.div(member, run)
        item = lax.rem(run_me + offset, groups) * run + lax.rem(member, run)
        return dp * item_size + item, {"dp": dp, "item": item}

    def each_peer(offset, act):
        @pl.loop(1 if offset == 0 else 0, members)
        def visit(j):
            member = lax.rem(member_me + j, members)
            peer, where = device(offset, member)
            act(member, peer, where)

    barrier = pltpu.get_barrier_semaphore()

    def greet(member, peer, where):
        pl.semaphore_signal(barrier, inc=1, device_id=where, device_id_type=pl.DeviceIdType.MESH)

    far_first = sorted(range(groups), key=lambda g: -min(g, groups - g))
    for offset in far_first:
        each_peer(offset, greet)

    loads = [
        pltpu.make_async_copy(source, target, load_sem.at[i])
        for i, (source, target) in enumerate(
            [
                (cand_hbm, cand_ref),
                (query_hbm, query_ref),
                (feature_hbm, feature_ref),
                (first_hbm, first),
                (table_hbm, table),
                (second_hbm, second_w),
                (score_hbm, score_ref),
                (length_hbm, length_ref),
                (slot_hbm, slot_ref),
                (prop_hbm, prop_ref),
            ]
        )
    ]
    for load in loads:
        load.start()
    loads[0].wait()

    ids = cand_ref[...]
    holder = lax.div(ids, item_rows)
    local = ids - holder * item_rows
    high = lax.div(local, LANES).astype(F32)
    low = lax.rem(local, LANES).astype(F32)
    held = (lax.broadcasted_iota(jnp.int32, (n, slots), 0) == holder).astype(F32)
    blocks = slots // LANES
    stacked = jnp.concatenate(
        [held[:, b * LANES : (b + 1) * LANES] for b in range(blocks)], axis=0
    ).astype(BF16)
    before = (
        lax.broadcasted_iota(jnp.int32, (LANES, LANES), 0)
        < lax.broadcasted_iota(jnp.int32, (LANES, LANES), 1)
    ).astype(F32)
    counter = jnp.concatenate([before, jnp.ones((LANES, LANES), F32)], axis=1).astype(BF16)
    counts = dot(stacked, counter, NN)
    total = jnp.zeros((n, LANES), F32)
    rank_parts = []
    for b in range(blocks):
        here = counts[b * n : (b + 1) * n]
        place = here[:, :LANES] + total
        rank_parts.append(
            jnp.sum(held[:, b * LANES : (b + 1) * LANES] * place, axis=0, keepdims=True)
        )
        total = total + here[:, LANES:]
    rank = jnp.concatenate(rank_parts, axis=1)
    at_rank = (
        lax.broadcasted_iota(jnp.int32, (LANES, slots), 0).astype(F32) == rank
    ).astype(F32)
    parts = jnp.concatenate([held * high, held * low], axis=0).astype(BF16)
    asked = dot(parts, at_rank.astype(BF16), NT)
    asked = (asked[:n] * float(LANES) + asked[n:]).astype(jnp.int32)
    tall = items.shape[1]
    scale = tall
    send_ids[:, 0, :] = jnp.clip(asked, 0, item_rows - 1) * scale

    for load in loads[1:4]:
        load.wait()
    context_part = dot(feature_ref[...], first[:feature_width, :], NN) * 0.5
    send1[0, :, :width] = query_ref[...].astype(F32)
    send1[0, :, width:] = context_part
    for load in loads[4:]:
        load.wait()
    second_w[...] = second_w[...] * jnp.asarray(0.5, BF16)

    flat = items.reshape(item_rows * tall, LANES)
    hidden_tiles = hidden_width // LANES
    step = math.gcd(256, item_rows)
    strips = item_rows // step
    early = strips * 4 // 8

    def project(start, stop):
        @pl.loop(start, stop)
        def visit(i):
            part = pl.ds(pl.multiple_of(i * step, step), step)
            block = table[part]
            projected = dot(block, first[feature_width:, :], NN) * 0.5
            base = pl.multiple_of(i * (step * tall), step * tall)

            def put(j, value):
                flat[pl.ds(base + j, step, stride=tall), :] = value

            for j in range(hidden_tiles):
                put(j, projected[:, j * LANES : (j + 1) * LANES])
            for j in range(width // LANES):
                put(hidden_tiles + j, block[:, j * LANES : (j + 1) * LANES].astype(F32))

    project(0, early)
    pl.semaphore_wait(barrier, n - 1)

    def ask(offset):
        seen = (groups - offset) % groups

        def act(member, peer, where):
            slot = pl.ds(seen * members + member_me, 1)
            pltpu.make_async_remote_copy(
                src_ref=send_ids.at[pl.ds(peer, 1)],
                dst_ref=wanted.at[slot],
                send_sem=send_sem.at[2],
                recv_sem=index_sem.at[seen],
                device_id=where,
                device_id_type=pl.DeviceIdType.MESH,
            ).start()
            pltpu.make_async_remote_copy(
                src_ref=send1,
                dst_ref=recv1.at[slot],
                send_sem=send_sem.at[0],
                recv_sem=arrive_sem.at[seen],
                device_id=where,
                device_id_type=pl.DeviceIdType.MESH,
            ).start()

        each_peer(offset, act)

    def give_back(group):
        offset = group

        @pl.loop(0, members)
        def visit(j):
            member = lax.rem(member_me + j, members)
            peer, where = device(offset, member)

            @pl.when(peer != me)
            def send():
                pltpu.make_async_remote_copy(
                    src_ref=send2.at[pl.ds(offset * members + member, 1)],
                    dst_ref=recv2.at[pl.ds(me, 1)],
                    send_sem=send_sem.at[1],
                    recv_sem=return_sem,
                    device_id=where,
                    device_id_type=pl.DeviceIdType.MESH,
                ).start()

    def wait_ids(group, expected):
        rows = wanted.at[pl.ds(group * members, expected)]
        pltpu.make_async_copy(
            send_ids.at[pl.ds(0, expected)], rows, index_sem.at[group]
        ).wait()

    def wait_rows(buffer, count, semaphore):
        rows = buffer.at[pl.ds(0, count)]
        pltpu.make_async_copy(rows, rows, semaphore).wait()

    for offset in far_first:
        ask(offset)
    own_ids = pltpu.make_async_copy(
        send_ids.at[pl.ds(me, 1)], wanted.at[pl.ds(member_me, 1)], own_sem.at[0]
    )
    own_ids.start()
    own_ask = pltpu.make_async_copy(send1, recv1.at[pl.ds(member_me, 1)], own_sem.at[1])
    own_ask.start()
    project(early, strips)
    own_ids.wait()
    own_ask.wait()

    lane = lax.broadcasted_iota(jnp.int32, (members, LANES), 1)
    row = lax.broadcasted_iota(jnp.int32, (members, LANES), 0)
    score_rows = jnp.broadcast_to(score_ref[...].reshape(1, hidden_width), (LANES, hidden_width))
    count = cap * members
    copies = LANES // members
    split = math.gcd(4, copies)
    part_rows = item_rows // split

    def rank_group(turn, group):
        rows_here = pl.ds(group * members, members)
        query = recv1[rows_here, 0, :width]
        context = recv1[rows_here, 0, width:]
        blank = jnp.zeros_like(query)
        logits = None
        for part in range(split):
            spread = jnp.concatenate(
                [query if j % split == part else blank for j in range(copies)], axis=0
            ).astype(BF16)
            partial = dot(table[part * part_rows : (part + 1) * part_rows], spread, NT)
            logits = partial if logits is None else logits + partial
        top = jnp.max(logits, axis=0, keepdims=True)
        turns = [members << k for k in range(split.bit_length() - 1)]
        for shift in turns:
            top = jnp.maximum(top, pltpu.roll(top, shift, 1))
        mass = jnp.sum(jnp.exp(logits - top), axis=0, keepdims=True)
        for shift in turns:
            mass = mass + pltpu.roll(mass, shift, 1)

        def own_lane(value):
            return jnp.sum(jnp.where(lane == row, value, 0.0), axis=1, keepdims=True)

        for r in range(cap):
            for c in range(members):
                at = wanted[group * members + c, 0, r]
                place = (turn * cap + r) * members + c
                found[pl.ds(place * tall, tall)] = flat[pl.ds(at, tall)]

        def found_tile(j):
            return found[pl.ds(turn * count * tall + j, count, stride=tall), :]

        item_part = jnp.concatenate([found_tile(j) for j in range(hidden_tiles)], axis=1)
        rows = jnp.concatenate(
            [found_tile(hidden_tiles + j) for j in range(width // LANES)], axis=1
        )
        half = item_part + jnp.concatenate([context] * cap, axis=0)
        hidden = (half + half * jnp.tanh(half)).astype(BF16)
        half = dot(hidden, second_w[...], NN)
        second = (half + half * jnp.tanh(half)).astype(BF16)
        score = dot(second, score_rows, NT)
        result = jnp.where(lane == max_at, own_lane(top), own_lane(mass))
        for r in range(cap):
            mine = slice(r * members, (r + 1) * members)
            gen = jnp.sum(rows[mine] * query, axis=1, keepdims=True)
            result = jnp.where(lane == r, score[mine], result)
            result = jnp.where(lane == gen_at + r, gen, result)
        send2[rows_here, 0, :] = result

    near_first = sorted(range(groups), key=lambda g: min(g, groups - g))
    order = near_first
    for turn, group in enumerate(order):
        expected = members - 1 if group == 0 else members
        wait_ids(group, expected)
        wait_rows(recv1, expected, arrive_sem.at[group])
        rank_group(turn, group)
        give_back(group)
    own_back = pltpu.make_async_copy(
        send2.at[pl.ds(member_me, 1)], recv2.at[pl.ds(me, 1)], own_sem.at[2]
    )
    own_back.start()
    own_back.wait()
    wait_rows(send_ids, n - 1, send_sem.at[2])
    wait_rows(recv1, n - 1, send_sem.at[0])
    wait_rows(recv2, n - 1, return_sem)

    back = recv2[:, 0, :]
    top = back.astype(BF16)
    rest = back - top.astype(F32)
    middle = rest.astype(BF16)
    bottom = (rest - middle.astype(F32)).astype(BF16)
    pieces = jnp.concatenate([top.astype(F32), middle.astype(F32), bottom.astype(F32)], axis=0)
    held_bf = held.astype(BF16)
    spread = dot(
        pieces.astype(BF16).T, jnp.concatenate([held_bf, held_bf, held_bf], axis=0), NN
    )
    score = jnp.sum(at_rank[:gen_at] * spread[:gen_at], axis=0, keepdims=True)
    gen = jnp.sum(at_rank[:gen_at] * spread[gen_at : 2 * gen_at], axis=0, keepdims=True)

    maxima = back[:, max_at : max_at + 1]
    sums = back[:, max_at + 1 : max_at + 2]
    peak = jnp.max(maxima, axis=0, keepdims=True)
    log_norm = peak + jnp.log(jnp.sum(sums * jnp.exp(maxima - peak), axis=0, keepdims=True))

    length = length_ref[0]
    position = lax.broadcasted_iota(jnp.int32, (1, slots), 1)
    live = position < length
    masked = jnp.where(live, score, -1e30)
    rank_peak = jnp.max(masked, axis=1, keepdims=True)
    rank_norm = rank_peak + jnp.log(
        jnp.sum(jnp.where(live, jnp.exp(masked - rank_peak), 0.0), axis=1, keepdims=True)
    )
    section = jnp.where(
        live, score - rank_norm + gen - log_norm + math.log(item_rows * n), 0.0
    )
    chosen = jnp.sum(jnp.where(position == slot_ref[0], section, 0.0), axis=1, keepdims=True)
    count = jnp.full((1, 1), length, jnp.int32).astype(F32)
    prop = jnp.full((1, 1), prop_ref[0], jnp.int32).astype(F32) / 1024.0
    section_ref[...] = section
    weight_ref[...] = chosen + jnp.log(count) - jnp.log(prop)
    wait_rows(send2, n - 1, send_sem.at[1])


def solution(mesh):
    dp_size, item_size = mesh.shape["dp"], mesh.shape["item"]
    n = dp_size * item_size

    def body(
        query,
        item_table,
        context_features,
        candidates,
        lengths,
        logged_slot,
        logging_prop,
        w_first,
        w_second,
        w_score,
    ):
        slots = candidates.shape[1]
        cap = max(2, 3 * slots // (2 * n))
        width = query.shape[1]
        hidden_width = w_first.shape[1]
        message = width + hidden_width
        tall = round_up((width + hidden_width) // LANES, 8)
        vmem = pl.BlockSpec(memory_space=pltpu.VMEM)
        groups = math.gcd(4, item_size)
        section, weight = pl.pallas_call(
            functools.partial(kernel, dp_size, item_size, groups, cap),
            out_shape=(
                pltpu.VMEM((1, slots), F32),
                pltpu.VMEM((1, 1), F32),
            ),
            in_specs=[pl.BlockSpec(memory_space=pltpu.HBM)] * 10,
            out_specs=(vmem, vmem),
            scratch_shapes=[
                pltpu.VMEM(query.shape, BF16),
                pltpu.VMEM(context_features.shape, BF16),
                pltpu.VMEM(candidates.shape, jnp.int32),
                pltpu.SMEM((1,), jnp.int32),
                pltpu.SMEM((1,), jnp.int32),
                pltpu.SMEM((1,), jnp.int32),
                pltpu.VMEM(w_score.shape, BF16),
                pltpu.VMEM(item_table.shape, BF16),
                pltpu.VMEM(w_first.shape, BF16),
                pltpu.VMEM(w_second.shape, BF16),
                pltpu.VMEM((n, 1, LANES), jnp.int32),
                pltpu.VMEM((1, 1, message), F32),
                pltpu.VMEM((n, 1, message), F32),
                pltpu.VMEM((n, 1, LANES), F32),
                pltpu.VMEM((n, 1, LANES), F32),
                pltpu.SemaphoreType.DMA((10,)),
                pltpu.SemaphoreType.DMA((3,)),
                pltpu.SemaphoreType.DMA((groups,)),
                pltpu.SemaphoreType.DMA((groups,)),
                pltpu.SemaphoreType.DMA,
                pltpu.SemaphoreType.DMA((3,)),
                pltpu.VMEM((item_table.shape[0], tall, LANES), F32),
                pltpu.VMEM((n * cap * tall + tall, LANES), F32),
                pltpu.SMEM((n, 1, LANES), jnp.int32),
            ],
            compiler_params=pltpu.CompilerParams(collective_id=0, has_side_effects=True),
            name="propensity",
        )(
            query,
            context_features,
            candidates,
            lengths,
            logged_slot,
            logging_prop,
            item_table,
            w_first,
            w_second,
            w_score,
        )
        return section, weight.reshape(-1)

    split = P(("dp", "item"))
    rows = P(("dp", "item"), None)
    return jax.shard_map(
        body,
        mesh=mesh,
        in_specs=(rows, rows, rows, rows, split, split, split, P(), P(), P()),
        out_specs=(rows, split),
        check_vma=False,
    )
```

```python
import functools
import math

import jax
import jax.numpy as jnp
from jax import lax
from jax.experimental import pallas as pl
from jax.experimental.pallas import tpu as pltpu
from jax.sharding import PartitionSpec as P

F32 = jnp.float32
BF16 = jnp.bfloat16
LANES = 128
NT = (((1,), (1,)), ((), ()))
NN = (((1,), (0,)), ((), ()))
TN = (((0,), (0,)), ((), ()))


def round_up(value, step):
    return (value + step - 1) // step * step


def dot(left, right, dims):
    return lax.dot_general(left, right, dims, preferred_element_type=F32)


def silu(v):
    half = v * 0.5
    return half + half * jnp.tanh(half)


def kernel(
    dp_size,
    item_size,
    groups,
    cap,
    query_hbm,
    feature_hbm,
    cand_hbm,
    length_hbm,
    slot_hbm,
    prop_hbm,
    table_hbm,
    first_hbm,
    second_hbm,
    score_hbm,
    section_ref,
    weight_ref,
    query_ref,
    feature_ref,
    cand_ref,
    length_ref,
    slot_ref,
    prop_ref,
    score_ref,
    table,
    first,
    second_w,
    send_ids,
    send1,
    recv1,
    send2,
    recv2,
    load_sem,
    send_sem,
    arrive_sem,
    index_sem,
    return_sem,
    own_sem,
    items,
    found,
    wanted,
):
    n = dp_size * item_size
    item_rows, width = table.shape
    slots = cand_ref.shape[1]
    feature_width = feature_ref.shape[1]
    hidden_width = first.shape[1]
    gen_at = round_up(cap, 8)
    max_at = 2 * gen_at
    dp_me, item_me = lax.axis_index("dp"), lax.axis_index("item")
    me = dp_me * item_size + item_me
    run = item_size // groups
    members = dp_size * run
    run_me = lax.div(item_me, run)
    member_me = dp_me * run + lax.rem(item_me, run)

    def device(offset, member):
        dp = lax.div(member, run)
        item = lax.rem(run_me + offset, groups) * run + lax.rem(member, run)
        return dp * item_size + item, {"dp": dp, "item": item}

    def each_peer(offset, act):
        @pl.loop(1 if isinstance(offset, int) else 0, members)
        def visit(j):
            member = lax.rem(member_me + j, members)
            peer, where = device(offset, member)
            act(member, peer, where)

    barrier = pltpu.get_barrier_semaphore()

    def greet(member, peer, where):
        pl.semaphore_signal(barrier, inc=1, device_id=where, device_id_type=pl.DeviceIdType.MESH)

    end = jnp.where(2 * run_me < groups, groups - 1, 0)
    far = lax.rem(end - run_me + groups, groups)
    middle = [jnp.where(far <= k, k + 1, k) for k in range(1, groups - 1)]
    far_first = ([far] if groups > 1 else []) + middle[::-1] + [0]
    for offset in far_first:
        each_peer(offset, greet)

    loads = [
        pltpu.make_async_copy(source, target, load_sem.at[i])
        for i, (source, target) in enumerate(
            [
                (cand_hbm, cand_ref),
                (query_hbm, query_ref),
                (feature_hbm, feature_ref),
                (first_hbm, first),
                (table_hbm, table),
                (second_hbm, second_w),
                (score_hbm, score_ref),
                (length_hbm, length_ref),
                (slot_hbm, slot_ref),
                (prop_hbm, prop_ref),
            ]
        )
    ]
    for load in loads:
        load.start()
    loads[0].wait()

    ids = cand_ref[...]
    holder = lax.div(ids, item_rows)
    local = ids - holder * item_rows
    high = lax.div(local, LANES).astype(F32)
    low = lax.rem(local, LANES).astype(F32)
    held = (lax.broadcasted_iota(jnp.int32, (n, slots), 0) == holder).astype(F32)
    blocks = slots // LANES
    stacked = jnp.concatenate(
        [held[:, b * LANES : (b + 1) * LANES] for b in range(blocks)], axis=0
    ).astype(BF16)
    before = (
        lax.broadcasted_iota(jnp.int32, (LANES, LANES), 0)
        < lax.broadcasted_iota(jnp.int32, (LANES, LANES), 1)
    ).astype(F32)
    counter = jnp.concatenate([before, jnp.ones((LANES, LANES), F32)], axis=1).astype(BF16)
    counts = dot(stacked, counter, NN)
    total = jnp.zeros((n, LANES), F32)
    rank_parts = []
    for b in range(blocks):
        here = counts[b * n : (b + 1) * n]
        place = here[:, :LANES] + total
        rank_parts.append(
            jnp.sum(held[:, b * LANES : (b + 1) * LANES] * place, axis=0, keepdims=True)
        )
        total = total + here[:, LANES:]
    rank = jnp.concatenate(rank_parts, axis=1)
    at_rank = (
        lax.broadcasted_iota(jnp.int32, (LANES, slots), 0).astype(F32) == rank
    ).astype(F32)
    parts = jnp.concatenate([held * high, held * low], axis=0).astype(BF16)
    asked = dot(parts, at_rank.astype(BF16), NT)
    asked = (asked[:n] * float(LANES) + asked[n:]).astype(jnp.int32)
    tall = items.shape[0] // item_rows
    lines = tall - 1
    scale = tall
    send_ids[:, 0, :] = jnp.clip(asked, 0, item_rows - 1) * scale

    for load in loads[1:4]:
        load.wait()
    context_part = dot(feature_ref[...], first[:feature_width, :], NN) * 0.5
    send1[0, :, :width] = query_ref[...].astype(F32)
    send1[0, :, width:] = context_part
    for load in loads[4:]:
        load.wait()
    second_w[...] = second_w[...] * jnp.asarray(0.5, BF16)

    hidden_tiles = hidden_width // LANES
    step = math.gcd(256, item_rows)
    strips = item_rows // step
    early = lax.div(strips * jnp.maximum(groups - 2 * run_me, 0), groups)

    def project(start, stop):
        @pl.loop(start, stop)
        def visit(i):
            part = pl.ds(pl.multiple_of(i * step, step), step)
            block = table[part]
            projected = dot(block, first[feature_width:, :], NN) * 0.5
            base = pl.multiple_of(i * (step * tall), step * tall)

            def put(j, value):
                items[pl.ds(base + j, step, stride=tall), :] = value

            for j in range(hidden_tiles):
                put(j, projected[:, j * LANES : (j + 1) * LANES])
            for j in range(width // LANES):
                put(hidden_tiles + j, block[:, j * LANES : (j + 1) * LANES].astype(F32))

    project(0, early)
    pl.semaphore_wait(barrier, n - 1)

    def ask(offset):
        seen = lax.rem(groups - offset, groups)

        def act(member, peer, where):
            slot = pl.ds(seen * members + member_me, 1)
            pltpu.make_async_remote_copy(
                src_ref=send_ids.at[pl.ds(peer, 1)],
                dst_ref=wanted.at[slot],
                send_sem=send_sem.at[2],
                recv_sem=index_sem.at[seen],
                device_id=where,
                device_id_type=pl.DeviceIdType.MESH,
            ).start()
            pltpu.make_async_remote_copy(
                src_ref=send1,
                dst_ref=recv1.at[slot],
                send_sem=send_sem.at[0],
                recv_sem=arrive_sem.at[seen],
                device_id=where,
                device_id_type=pl.DeviceIdType.MESH,
            ).start()

        each_peer(offset, act)

    def give_back(group):
        offset = group

        @pl.loop(0, members)
        def visit(j):
            member = lax.rem(member_me + j, members)
            peer, where = device(offset, member)

            @pl.when(peer != me)
            def send():
                pltpu.make_async_remote_copy(
                    src_ref=send2.at[pl.ds(offset * members + member, 1)],
                    dst_ref=recv2.at[pl.ds(me, 1)],
                    send_sem=send_sem.at[1],
                    recv_sem=return_sem,
                    device_id=where,
                    device_id_type=pl.DeviceIdType.MESH,
                ).start()

    def wait_ids(group, expected):
        rows = wanted.at[pl.ds(group * members, expected)]
        pltpu.make_async_copy(
            send_ids.at[pl.ds(0, expected)], rows, index_sem.at[group]
        ).wait()

    def wait_rows(buffer, count, semaphore):
        rows = buffer.at[pl.ds(0, count)]
        pltpu.make_async_copy(rows, rows, semaphore).wait()

    for offset in (far_first[:1] + far_first[:0:-1]):
        ask(offset)
    own_ids = pltpu.make_async_copy(
        send_ids.at[pl.ds(me, 1)], wanted.at[pl.ds(member_me, 1)], own_sem.at[0]
    )
    own_ids.start()
    own_ask = pltpu.make_async_copy(send1, recv1.at[pl.ds(member_me, 1)], own_sem.at[1])
    own_ask.start()
    project(early, strips)
    own_ids.wait()
    own_ask.wait()

    lane = lax.broadcasted_iota(jnp.int32, (members, LANES), 1)
    score_row = score_ref[...].reshape(1, hidden_width).astype(F32)
    copies = max(1, LANES // n)
    split = 1 << (math.gcd(4, copies).bit_length() - 1)
    part_rows = item_rows // split

    def rank_groups(turn, batch):
        count = cap * members * len(batch)
        base = turn * cap * members
        for r in range(cap):
            for b, group in enumerate(batch):
                for c in range(members):
                    at = wanted[group * members + c, 0, r]
                    place = base + (r * len(batch) + b) * members + c
                    found[pl.ds(place * tall, lines)] = items[pl.ds(at, lines)]

        def found_tile(j):
            return found[pl.ds(base * tall + j, count, stride=tall), :]

        def stacked_rows(low, high):
            return jnp.concatenate(
                [recv1[pl.ds(group * members, members), 0, low:high] for group in batch], axis=0
            )

        query = stacked_rows(0, width)
        context = stacked_rows(width, width + hidden_width)
        item_part = jnp.concatenate([found_tile(j) for j in range(hidden_tiles)], axis=1)
        rows = jnp.concatenate(
            [found_tile(hidden_tiles + j) for j in range(width // LANES)], axis=1
        )
        half = item_part + jnp.concatenate([context] * cap, axis=0)
        hidden = (half + half * jnp.tanh(half)).astype(BF16)
        half = dot(hidden, second_w[...], NN)
        second = (half + half * jnp.tanh(half)).astype(BF16).astype(F32) * score_row
        deep = len(batch) * members
        lanes = lax.broadcasted_iota(jnp.int32, (deep, LANES), 1)
        result = jnp.zeros((deep, LANES), F32)
        for r in range(cap):
            mine = slice(r * deep, (r + 1) * deep)
            score = jnp.sum(second[mine], axis=1, keepdims=True)
            gen = jnp.sum(rows[mine] * query, axis=1, keepdims=True)
            result = jnp.where(lanes == r, score, result)
            result = jnp.where(lanes == gen_at + r, gen, result)
        for b, group in enumerate(batch):
            send2[pl.ds(group * members, members), 0, :] = result[
                b * members : (b + 1) * members
            ]

    def normalizers():
        query = recv1[:, 0, :width]
        blank = jnp.zeros_like(query)
        logits = None
        for part in range(split):
            spread = jnp.concatenate(
                [query if j % split == part else blank for j in range(copies)], axis=0
            ).astype(BF16)
            partial = dot(table[part * part_rows : (part + 1) * part_rows], spread, NT)
            logits = partial if logits is None else logits + partial
        top = jnp.max(logits, axis=0, keepdims=True)
        mass = jnp.sum(jnp.exp(logits - top), axis=0, keepdims=True)
        peak = top
        shifts = [n << k for k in range(split.bit_length() - 1)]
        for shift in shifts:
            peak = jnp.maximum(peak, pltpu.roll(peak, shift, 1))
        mass = mass * jnp.exp(top - peak)
        for shift in shifts:
            mass = mass + pltpu.roll(mass, shift, 1)
        return peak, mass

    def finish(group, peak, mass):
        rows_here = pl.ds(group * members, members)
        across = (members, peak.shape[1])
        mine = lax.broadcasted_iota(jnp.int32, across, 1) == group * members + (
            lax.broadcasted_iota(jnp.int32, across, 0)
        )

        def own_lane(value):
            return jnp.sum(jnp.where(mine, value, 0.0), axis=1, keepdims=True)

        result = jnp.where(lane == max_at, own_lane(peak), send2[rows_here, 0, :])
        send2[rows_here, 0, :] = jnp.where(lane == max_at + 1, own_lane(mass), result)

    batches = [batch for batch in ([0], middle, far_first[:-1][:1]) if batch]
    once = 1 + lax.div(me, n)
    turn = 0
    for batch in batches:
        @pl.loop(0, once)
        def arrive(_, batch=batch):
            for group in batch:
                expected = members - 1 if isinstance(group, int) else members
                wait_ids(group, expected)
                wait_rows(recv1, expected, arrive_sem.at[group])

        if batch is batches[-1]:
            peak, mass = normalizers()
        rank_groups(turn, batch)
        turn += len(batch)
    for batch in reversed(batches):
        for group in batch:
            finish(group, peak, mass)
            give_back(group)
    own_back = pltpu.make_async_copy(
        send2.at[pl.ds(member_me, 1)], recv2.at[pl.ds(me, 1)], own_sem.at[2]
    )
    own_back.start()
    own_back.wait()
    wait_rows(send_ids, n - 1, send_sem.at[2])
    wait_rows(recv1, n - 1, send_sem.at[0])
    wait_rows(recv2, n - 1, return_sem)

    back = recv2[:, 0, :]
    top = back.astype(BF16)
    rest = back - top.astype(F32)
    middle = rest.astype(BF16)
    bottom = (rest - middle.astype(F32)).astype(BF16)
    pieces = jnp.concatenate([top.astype(F32), middle.astype(F32), bottom.astype(F32)], axis=0)
    held_bf = held.astype(BF16)
    spread = dot(
        pieces.astype(BF16).T, jnp.concatenate([held_bf, held_bf, held_bf], axis=0), NN
    )
    score = jnp.sum(at_rank[:gen_at] * spread[:gen_at], axis=0, keepdims=True)
    gen = jnp.sum(at_rank[:gen_at] * spread[gen_at : 2 * gen_at], axis=0, keepdims=True)

    maxima = back[:, max_at : max_at + 1]
    sums = back[:, max_at + 1 : max_at + 2]
    peak = jnp.max(maxima, axis=0, keepdims=True)
    log_norm = peak + jnp.log(jnp.sum(sums * jnp.exp(maxima - peak), axis=0, keepdims=True))

    length = length_ref[0]
    position = lax.broadcasted_iota(jnp.int32, (1, slots), 1)
    live = position < length
    masked = jnp.where(live, score, -1e30)
    rank_peak = jnp.max(masked, axis=1, keepdims=True)
    rank_norm = rank_peak + jnp.log(
        jnp.sum(jnp.where(live, jnp.exp(masked - rank_peak), 0.0), axis=1, keepdims=True)
    )
    section = jnp.where(
        live, score - rank_norm + gen - log_norm + math.log(item_rows * n), 0.0
    )
    chosen = jnp.sum(jnp.where(position == slot_ref[0], section, 0.0), axis=1, keepdims=True)
    count = jnp.full((1, 1), length, jnp.int32).astype(F32)
    prop = jnp.full((1, 1), prop_ref[0], jnp.int32).astype(F32) / 1024.0
    section_ref[...] = section
    weight_ref[...] = chosen + jnp.log(count) - jnp.log(prop)
    wait_rows(send2, n - 1, send_sem.at[1])


def solution(mesh):
    dp_size, item_size = mesh.shape["dp"], mesh.shape["item"]
    n = dp_size * item_size

    def body(
        query,
        item_table,
        context_features,
        candidates,
        lengths,
        logged_slot,
        logging_prop,
        w_first,
        w_second,
        w_score,
    ):
        slots = candidates.shape[1]
        cap = max(2, 3 * slots // (2 * n))
        width = query.shape[1]
        hidden_width = w_first.shape[1]
        message = width + hidden_width
        tall = round_up((width + hidden_width) // LANES, 8) + 1
        vmem = pl.BlockSpec(memory_space=pltpu.VMEM)
        groups = math.gcd(4, item_size)
        section, weight = pl.pallas_call(
            functools.partial(kernel, dp_size, item_size, groups, cap),
            out_shape=(
                pltpu.VMEM((1, slots), F32),
                pltpu.VMEM((1, 1), F32),
            ),
            in_specs=[pl.BlockSpec(memory_space=pltpu.HBM)] * 10,
            out_specs=(vmem, vmem),
            scratch_shapes=[
                pltpu.VMEM(query.shape, BF16),
                pltpu.VMEM(context_features.shape, BF16),
                pltpu.VMEM(candidates.shape, jnp.int32),
                pltpu.SMEM((1,), jnp.int32),
                pltpu.SMEM((1,), jnp.int32),
                pltpu.SMEM((1,), jnp.int32),
                pltpu.VMEM(w_score.shape, BF16),
                pltpu.VMEM(item_table.shape, BF16),
                pltpu.VMEM(w_first.shape, BF16),
                pltpu.VMEM(w_second.shape, BF16),
                pltpu.VMEM((n, 1, LANES), jnp.int32),
                pltpu.VMEM((1, 1, message), F32),
                pltpu.VMEM((n, 1, message), F32),
                pltpu.VMEM((n, 1, LANES), F32),
                pltpu.VMEM((n, 1, LANES), F32),
                pltpu.SemaphoreType.DMA((10,)),
                pltpu.SemaphoreType.DMA((3,)),
                pltpu.SemaphoreType.DMA((groups,)),
                pltpu.SemaphoreType.DMA((groups,)),
                pltpu.SemaphoreType.DMA,
                pltpu.SemaphoreType.DMA((3,)),
                pltpu.VMEM((item_table.shape[0] * tall, LANES), F32),
                pltpu.VMEM((n * cap * tall + tall, LANES), F32),
                pltpu.SMEM((n, 1, LANES), jnp.int32),
            ],
            compiler_params=pltpu.CompilerParams(collective_id=0, has_side_effects=True),
            name="propensity",
        )(
            query,
            context_features,
            candidates,
            lengths,
            logged_slot,
            logging_prop,
            item_table,
            w_first,
            w_second,
            w_score,
        )
        return section, weight.reshape(-1)

    split = P(("dp", "item"))
    rows = P(("dp", "item"), None)
    return jax.shard_map(
        body,
        mesh=mesh,
        in_specs=(rows, rows, rows, rows, split, split, split, P(), P(), P()),
        out_specs=(rows, split),
        check_vma=False,
    )
```

```python
import functools
import math

import jax
import jax.numpy as jnp
from jax import lax
from jax.experimental import pallas as pl
from jax.experimental.pallas import tpu as pltpu
from jax.sharding import PartitionSpec as P

F32 = jnp.float32
BF16 = jnp.bfloat16
LANES = 128
NT = (((1,), (1,)), ((), ()))
NN = (((1,), (0,)), ((), ()))
TN = (((0,), (0,)), ((), ()))


def round_up(value, step):
    return (value + step - 1) // step * step


def dot(left, right, dims):
    return lax.dot_general(left, right, dims, preferred_element_type=F32)


def silu(v):
    half = v * 0.5
    return half + half * jnp.tanh(half)


def kernel(
    dp_size,
    item_size,
    groups,
    cap,
    query_hbm,
    feature_hbm,
    cand_hbm,
    length_hbm,
    slot_hbm,
    prop_hbm,
    table_hbm,
    first_hbm,
    second_hbm,
    score_hbm,
    section_ref,
    weight_ref,
    query_ref,
    feature_ref,
    cand_ref,
    length_ref,
    slot_ref,
    prop_ref,
    score_ref,
    table,
    first,
    second_w,
    send_ids,
    send1,
    recv1,
    send2,
    recv2,
    load_sem,
    send_sem,
    arrive_sem,
    index_sem,
    return_sem,
    own_sem,
    items,
    found,
    wanted,
):
    n = dp_size * item_size
    item_rows, width = table.shape
    slots = cand_ref.shape[1]
    feature_width = feature_ref.shape[1]
    hidden_width = first.shape[1]
    gen_at = round_up(cap, 8)
    max_at = 2 * gen_at
    dp_me, item_me = lax.axis_index("dp"), lax.axis_index("item")
    me = dp_me * item_size + item_me
    run = item_size // groups
    members = dp_size * run
    run_me = lax.div(item_me, run)
    member_me = dp_me * run + lax.rem(item_me, run)

    def device(offset, member):
        dp = lax.div(member, run)
        item = lax.rem(run_me + offset, groups) * run + lax.rem(member, run)
        return dp * item_size + item, {"dp": dp, "item": item}

    def each_peer(offset, act):
        @pl.loop(1 if isinstance(offset, int) else 0, members)
        def visit(j):
            member = lax.rem(member_me + j, members)
            peer, where = device(offset, member)
            act(member, peer, where)

    barrier = pltpu.get_barrier_semaphore()

    def greet(member, peer, where):
        pl.semaphore_signal(barrier, inc=1, device_id=where, device_id_type=pl.DeviceIdType.MESH)

    def farthest(plane):
        end = jnp.where(2 * plane < groups, groups - 1, 0)
        return lax.rem(end - plane + groups, groups)

    def turn_at(plane, offset):
        far = farthest(plane)
        place = offset - 1 - jnp.where(offset > far, 1, 0)
        place = jnp.where(2 * plane < groups, groups - 3 - place, place)
        return jnp.where(offset == far, 1, 2 + place)

    far = farthest(run_me)
    rising = [jnp.where(far <= k, k + 1, k) for k in range(1, groups - 1)]
    middle = [
        jnp.where(2 * run_me < groups, down, up) for up, down in zip(rising, rising[::-1])
    ]
    offsets = [0] + ([far] if groups > 1 else []) + middle
    far_first = offsets[1:] + [0]

    cand_load = pltpu.make_async_copy(cand_hbm, cand_ref, load_sem.at[0])
    cand_load.start()
    for offset in far_first:
        each_peer(offset, greet)

    loads = [
        pltpu.make_async_copy(source, target, load_sem.at[i + 1])
        for i, (source, target) in enumerate(
            [
                (query_hbm, query_ref),
                (feature_hbm, feature_ref),
                (first_hbm, first),
                (table_hbm, table),
                (second_hbm, second_w),
                (score_hbm, score_ref),
                (length_hbm, length_ref),
                (slot_hbm, slot_ref),
                (prop_hbm, prop_ref),
            ]
        )
    ]
    for load in loads:
        load.start()
    cand_load.wait()

    ids = cand_ref[...]
    holder = lax.div(ids, item_rows)
    local = ids - holder * item_rows
    high = lax.div(local, LANES).astype(F32)
    low = lax.rem(local, LANES).astype(F32)
    held = (lax.broadcasted_iota(jnp.int32, (n, slots), 0) == holder).astype(F32)
    blocks = slots // LANES
    stacked = jnp.concatenate(
        [held[:, b * LANES : (b + 1) * LANES] for b in range(blocks)], axis=0
    ).astype(BF16)
    before = (
        lax.broadcasted_iota(jnp.int32, (LANES, LANES), 0)
        < lax.broadcasted_iota(jnp.int32, (LANES, LANES), 1)
    ).astype(F32)
    counter = jnp.concatenate([before, jnp.ones((LANES, LANES), F32)], axis=1).astype(BF16)
    counts = dot(stacked, counter, NN)
    total = jnp.zeros((n, LANES), F32)
    rank_parts = []
    for b in range(blocks):
        here = counts[b * n : (b + 1) * n]
        place = here[:, :LANES] + total
        rank_parts.append(
            jnp.sum(held[:, b * LANES : (b + 1) * LANES] * place, axis=0, keepdims=True)
        )
        total = total + here[:, LANES:]
    rank = jnp.concatenate(rank_parts, axis=1)
    at_rank = (
        lax.broadcasted_iota(jnp.int32, (LANES, slots), 0).astype(F32) == rank
    ).astype(F32)
    parts = jnp.concatenate([held * high, held * low], axis=0).astype(BF16)
    asked = dot(parts, at_rank.astype(BF16), NT)
    asked = (asked[:n] * float(LANES) + asked[n:]).astype(jnp.int32)
    tall = items.shape[0] // item_rows
    lines = tall - 1
    scale = tall
    send_ids[:, 0, :] = jnp.clip(asked, 0, item_rows - 1) * scale

    for load in loads[:3]:
        load.wait()
    context_part = dot(feature_ref[...], first[:feature_width, :], NN) * 0.5
    send1[0, :, :width] = query_ref[...].astype(F32)
    send1[0, :, width:] = context_part
    for load in loads[3:]:
        load.wait()

    hidden_tiles = hidden_width // LANES
    step = math.gcd(256, item_rows)
    strips = item_rows // step
    early = lax.div(strips * jnp.maximum(groups - 2 * run_me, 0), 2 * groups)

    def project(start, stop):
        @pl.loop(start, stop)
        def visit(i):
            part = pl.ds(pl.multiple_of(i * step, step), step)
            block = table[part]
            projected = dot(block, first[feature_width:, :], NN) * 0.5
            base = pl.multiple_of(i * (step * tall), step * tall)

            def put(j, value):
                items[pl.ds(base + j, step, stride=tall), :] = value

            for j in range(hidden_tiles):
                put(j, projected[:, j * LANES : (j + 1) * LANES])
            for j in range(width // LANES):
                put(hidden_tiles + j, block[:, j * LANES : (j + 1) * LANES].astype(F32))

    project(0, early)
    pl.semaphore_wait(barrier, n - 1)

    def ask(offset):
        if isinstance(offset, int):
            seen = 0
        else:
            plane = lax.rem(run_me + offset, groups)
            seen = turn_at(plane, groups - offset)

        def act(member, peer, where):
            slot = pl.ds(seen * members + member_me, 1)
            pltpu.make_async_remote_copy(
                src_ref=send_ids.at[pl.ds(peer, 1)],
                dst_ref=wanted.at[slot],
                send_sem=send_sem.at[2],
                recv_sem=index_sem.at[seen],
                device_id=where,
                device_id_type=pl.DeviceIdType.MESH,
            ).start()
            pltpu.make_async_remote_copy(
                src_ref=send1,
                dst_ref=recv1.at[slot],
                send_sem=send_sem.at[0],
                recv_sem=arrive_sem.at[seen],
                device_id=where,
                device_id_type=pl.DeviceIdType.MESH,
            ).start()

        each_peer(offset, act)

    def give_back(turn):
        def act(member, peer, where):
            pltpu.make_async_remote_copy(
                src_ref=send2.at[pl.ds(turn * members + member, 1)],
                dst_ref=recv2.at[pl.ds(me, 1)],
                send_sem=send_sem.at[1],
                recv_sem=return_sem,
                device_id=where,
                device_id_type=pl.DeviceIdType.MESH,
            ).start()

        each_peer(offsets[turn], act)

    def wait_ids(group, expected):
        rows = wanted.at[pl.ds(group * members, expected)]
        pltpu.make_async_copy(
            send_ids.at[pl.ds(0, expected)], rows, index_sem.at[group]
        ).wait()

    def wait_rows(buffer, count, semaphore):
        rows = buffer.at[pl.ds(0, count)]
        pltpu.make_async_copy(rows, rows, semaphore).wait()

    for offset in (offsets[1:2] + [0] + offsets[2:]):
        ask(offset)
    own_ids = pltpu.make_async_copy(
        send_ids.at[pl.ds(me, 1)], wanted.at[pl.ds(member_me, 1)], own_sem.at[0]
    )
    own_ids.start()
    own_ask = pltpu.make_async_copy(send1, recv1.at[pl.ds(member_me, 1)], own_sem.at[1])
    own_ask.start()
    second_w[...] = second_w[...] * jnp.asarray(0.5, BF16)
    project(early, strips)
    own_ids.wait()
    own_ask.wait()

    lane = lax.broadcasted_iota(jnp.int32, (members, LANES), 1)
    score_row = score_ref[...].reshape(1, hidden_width).astype(F32)
    copies = max(1, LANES // n)
    split = 1 << (math.gcd(4, copies).bit_length() - 1)
    part_rows = item_rows // split

    def rank_groups(turn, batch):
        count = cap * members * len(batch)
        base = turn * cap * members
        for r in range(cap):
            for b, group in enumerate(batch):
                for c in range(members):
                    at = wanted[group * members + c, 0, r]
                    place = base + (r * len(batch) + b) * members + c
                    found[pl.ds(place * tall, lines)] = items[pl.ds(at, lines)]

        def found_tile(j):
            return found[pl.ds(base * tall + j, count, stride=tall), :]

        def stacked_rows(low, high):
            return jnp.concatenate(
                [recv1[pl.ds(group * members, members), 0, low:high] for group in batch], axis=0
            )

        query = stacked_rows(0, width)
        context = stacked_rows(width, width + hidden_width)
        item_part = jnp.concatenate([found_tile(j) for j in range(hidden_tiles)], axis=1)
        rows = jnp.concatenate(
            [found_tile(hidden_tiles + j) for j in range(width // LANES)], axis=1
        )
        half = item_part + jnp.concatenate([context] * cap, axis=0)
        hidden = (half + half * jnp.tanh(half)).astype(BF16)
        half = dot(hidden, second_w[...], NN)
        second = (half + half * jnp.tanh(half)).astype(BF16).astype(F32) * score_row
        deep = len(batch) * members
        lanes = lax.broadcasted_iota(jnp.int32, (deep, LANES), 1)
        result = jnp.zeros((deep, LANES), F32)
        for r in range(cap):
            mine = slice(r * deep, (r + 1) * deep)
            score = jnp.sum(second[mine], axis=1, keepdims=True)
            gen = jnp.sum(rows[mine] * query, axis=1, keepdims=True)
            result = jnp.where(lanes == r, score, result)
            result = jnp.where(lanes == gen_at + r, gen, result)
        for b, group in enumerate(batch):
            send2[pl.ds(group * members, members), 0, :] = result[
                b * members : (b + 1) * members
            ]

    def normalizers():
        query = recv1[:, 0, :width]
        blank = jnp.zeros_like(query)
        logits = None
        for part in range(split):
            spread = jnp.concatenate(
                [query if j % split == part else blank for j in range(copies)], axis=0
            ).astype(BF16)
            partial = dot(table[part * part_rows : (part + 1) * part_rows], spread, NT)
            logits = partial if logits is None else logits + partial
        top = jnp.max(logits, axis=0, keepdims=True)
        mass = jnp.sum(jnp.exp(logits - top), axis=0, keepdims=True)
        peak = top
        shifts = [n << k for k in range(split.bit_length() - 1)]
        for shift in shifts:
            peak = jnp.maximum(peak, pltpu.roll(peak, shift, 1))
        mass = mass * jnp.exp(top - peak)
        for shift in shifts:
            mass = mass + pltpu.roll(mass, shift, 1)
        return peak, mass

    def finish(group, peak, mass):
        rows_here = pl.ds(group * members, members)
        across = (members, peak.shape[1])
        mine = lax.broadcasted_iota(jnp.int32, across, 1) == group * members + (
            lax.broadcasted_iota(jnp.int32, across, 0)
        )

        def own_lane(value):
            return jnp.sum(jnp.where(mine, value, 0.0), axis=1, keepdims=True)

        result = jnp.where(lane == max_at, own_lane(peak), send2[rows_here, 0, :])
        send2[rows_here, 0, :] = jnp.where(lane == max_at + 1, own_lane(mass), result)

    once = 1 + lax.div(me, n)

    def arrive(turns):
        @pl.loop(0, once)
        def check(_):
            for turn in turns:
                expected = members if turn else members - 1
                wait_ids(turn, expected)
                wait_rows(recv1, expected, arrive_sem.at[turn])

    arrive([0])
    rank_groups(0, [0])
    others = list(range(1, groups))
    arrive(others)
    peak, mass = normalizers()
    for turn in others + [0]:
        if turn:
            rank_groups(turn, [turn])
        finish(turn, peak, mass)
        give_back(turn)
    own_back = pltpu.make_async_copy(
        send2.at[pl.ds(member_me, 1)], recv2.at[pl.ds(me, 1)], own_sem.at[2]
    )
    own_back.start()
    own_back.wait()
    wait_rows(send_ids, n - 1, send_sem.at[2])
    wait_rows(recv1, n - 1, send_sem.at[0])
    wait_rows(recv2, n - 1, return_sem)

    back = recv2[:, 0, :]
    top = back.astype(BF16)
    rest = back - top.astype(F32)
    middle = rest.astype(BF16)
    bottom = (rest - middle.astype(F32)).astype(BF16)
    pieces = jnp.concatenate([top.astype(F32), middle.astype(F32), bottom.astype(F32)], axis=0)
    held_bf = held.astype(BF16)
    spread = dot(
        pieces.astype(BF16).T, jnp.concatenate([held_bf, held_bf, held_bf], axis=0), NN
    )
    score = jnp.sum(at_rank[:gen_at] * spread[:gen_at], axis=0, keepdims=True)
    gen = jnp.sum(at_rank[:gen_at] * spread[gen_at : 2 * gen_at], axis=0, keepdims=True)

    maxima = back[:, max_at : max_at + 1]
    sums = back[:, max_at + 1 : max_at + 2]
    peak = jnp.max(maxima, axis=0, keepdims=True)
    log_norm = peak + jnp.log(jnp.sum(sums * jnp.exp(maxima - peak), axis=0, keepdims=True))

    length = length_ref[0]
    position = lax.broadcasted_iota(jnp.int32, (1, slots), 1)
    live = position < length
    masked = jnp.where(live, score, -1e30)
    rank_peak = jnp.max(masked, axis=1, keepdims=True)
    rank_norm = rank_peak + jnp.log(
        jnp.sum(jnp.where(live, jnp.exp(masked - rank_peak), 0.0), axis=1, keepdims=True)
    )
    section = jnp.where(
        live, score - rank_norm + gen - log_norm + math.log(item_rows * n), 0.0
    )
    chosen = jnp.sum(jnp.where(position == slot_ref[0], section, 0.0), axis=1, keepdims=True)
    count = jnp.full((1, 1), length, jnp.int32).astype(F32)
    prop = jnp.full((1, 1), prop_ref[0], jnp.int32).astype(F32) / 1024.0
    section_ref[...] = section
    weight_ref[...] = chosen + jnp.log(count) - jnp.log(prop)
    wait_rows(send2, n - 1, send_sem.at[1])


def solution(mesh):
    dp_size, item_size = mesh.shape["dp"], mesh.shape["item"]
    n = dp_size * item_size

    def body(
        query,
        item_table,
        context_features,
        candidates,
        lengths,
        logged_slot,
        logging_prop,
        w_first,
        w_second,
        w_score,
    ):
        slots = candidates.shape[1]
        cap = max(2, 3 * slots // (2 * n))
        width = query.shape[1]
        hidden_width = w_first.shape[1]
        message = width + hidden_width
        tall = round_up((width + hidden_width) // LANES, 8) + 1
        vmem = pl.BlockSpec(memory_space=pltpu.VMEM)
        groups = math.gcd(4, item_size)
        section, weight = pl.pallas_call(
            functools.partial(kernel, dp_size, item_size, groups, cap),
            out_shape=(
                pltpu.VMEM((1, slots), F32),
                pltpu.VMEM((1, 1), F32),
            ),
            in_specs=[pl.BlockSpec(memory_space=pltpu.HBM)] * 10,
            out_specs=(vmem, vmem),
            scratch_shapes=[
                pltpu.VMEM(query.shape, BF16),
                pltpu.VMEM(context_features.shape, BF16),
                pltpu.VMEM(candidates.shape, jnp.int32),
                pltpu.SMEM((1,), jnp.int32),
                pltpu.SMEM((1,), jnp.int32),
                pltpu.SMEM((1,), jnp.int32),
                pltpu.VMEM(w_score.shape, BF16),
                pltpu.VMEM(item_table.shape, BF16),
                pltpu.VMEM(w_first.shape, BF16),
                pltpu.VMEM(w_second.shape, BF16),
                pltpu.VMEM((n, 1, LANES), jnp.int32),
                pltpu.VMEM((1, 1, message), F32),
                pltpu.VMEM((n, 1, message), F32),
                pltpu.VMEM((n, 1, LANES), F32),
                pltpu.VMEM((n, 1, LANES), F32),
                pltpu.SemaphoreType.DMA((10,)),
                pltpu.SemaphoreType.DMA((3,)),
                pltpu.SemaphoreType.DMA((groups,)),
                pltpu.SemaphoreType.DMA((groups,)),
                pltpu.SemaphoreType.DMA,
                pltpu.SemaphoreType.DMA((3,)),
                pltpu.VMEM((item_table.shape[0] * tall, LANES), F32),
                pltpu.VMEM((n * cap * tall + tall, LANES), F32),
                pltpu.SMEM((n, 1, LANES), jnp.int32),
            ],
            compiler_params=pltpu.CompilerParams(collective_id=0, has_side_effects=True),
            name="propensity",
        )(
            query,
            context_features,
            candidates,
            lengths,
            logged_slot,
            logging_prop,
            item_table,
            w_first,
            w_second,
            w_score,
        )
        return section, weight.reshape(-1)

    split = P(("dp", "item"))
    rows = P(("dp", "item"), None)
    return jax.shard_map(
        body,
        mesh=mesh,
        in_specs=(rows, rows, rows, rows, split, split, split, P(), P(), P()),
        out_specs=(rows, split),
        check_vma=False,
    )
```

```python
import functools
import math

import jax
import jax.numpy as jnp
from jax import lax
from jax.experimental import pallas as pl
from jax.experimental.pallas import tpu as pltpu
from jax.sharding import PartitionSpec as P

F32 = jnp.float32
BF16 = jnp.bfloat16
LANES = 128
NT = (((1,), (1,)), ((), ()))
NN = (((1,), (0,)), ((), ()))
TN = (((0,), (0,)), ((), ()))


def round_up(value, step):
    return (value + step - 1) // step * step


def dot(left, right, dims):
    return lax.dot_general(left, right, dims, preferred_element_type=F32)


def silu(v):
    half = v * 0.5
    return half + half * jnp.tanh(half)


def kernel(
    dp_size,
    item_size,
    groups,
    cap,
    query_hbm,
    feature_hbm,
    cand_hbm,
    length_hbm,
    slot_hbm,
    prop_hbm,
    table_hbm,
    first_hbm,
    second_hbm,
    score_hbm,
    section_ref,
    weight_ref,
    query_ref,
    feature_ref,
    cand_ref,
    length_ref,
    slot_ref,
    prop_ref,
    score_ref,
    table,
    first,
    second_w,
    send_ids,
    send1,
    recv1,
    send2,
    recv2,
    load_sem,
    send_sem,
    arrive_sem,
    index_sem,
    return_sem,
    own_sem,
    items,
    found,
    wanted,
    tile_ref,
):
    n = dp_size * item_size
    item_rows, width = table.shape
    slots = cand_ref.shape[1]
    feature_width = feature_ref.shape[1]
    hidden_width = first.shape[1]
    gen_at = round_up(cap, 8)
    max_at = 2 * gen_at
    dp_me, item_me = lax.axis_index("dp"), lax.axis_index("item")
    me = dp_me * item_size + item_me
    run = item_size // groups
    members = dp_size * run
    run_me = lax.div(item_me, run)
    member_me = dp_me * run + lax.rem(item_me, run)

    def device(offset, member):
        dp = lax.div(member, run)
        item = lax.rem(run_me + offset, groups) * run + lax.rem(member, run)
        return dp * item_size + item, {"dp": dp, "item": item}

    def each_peer(offset, act):
        @pl.loop(1 if isinstance(offset, int) else 0, members)
        def visit(j):
            member = lax.rem(member_me + j, members)
            peer, where = device(offset, member)
            act(member, peer, where)

    barrier = pltpu.get_barrier_semaphore()

    def greet(member, peer, where):
        pl.semaphore_signal(barrier, inc=1, device_id=where, device_id_type=pl.DeviceIdType.MESH)

    def farthest(plane):
        end = jnp.where(2 * plane < groups, groups - 1, 0)
        return lax.rem(end - plane + groups, groups)

    def turn_at(plane, offset):
        far = farthest(plane)
        place = offset - 1 - jnp.where(offset > far, 1, 0)
        place = jnp.where(2 * plane < groups, groups - 3 - place, place)
        return jnp.where(offset == far, 1, 2 + place)

    far = farthest(run_me)
    rising = [jnp.where(far <= k, k + 1, k) for k in range(1, groups - 1)]
    middle = [
        jnp.where(2 * run_me < groups, down, up) for up, down in zip(rising, rising[::-1])
    ]
    offsets = [0] + ([far] if groups > 1 else []) + middle
    far_first = offsets[1:] + [0]

    cand_load = pltpu.make_async_copy(cand_hbm, cand_ref, load_sem.at[0])
    cand_load.start()
    for offset in far_first:
        each_peer(offset, greet)

    loads = [
        pltpu.make_async_copy(source, target, load_sem.at[i + 1])
        for i, (source, target) in enumerate(
            [
                (query_hbm, query_ref),
                (feature_hbm, feature_ref),
                (first_hbm, first),
                (table_hbm, table),
                (second_hbm, second_w),
                (score_hbm, score_ref),
                (length_hbm, length_ref),
                (slot_hbm, slot_ref),
                (prop_hbm, prop_ref),
            ]
        )
    ]
    for load in loads:
        load.start()
    cand_load.wait()

    ids = cand_ref[...]
    holder = lax.div(ids, item_rows)
    local = ids - holder * item_rows
    high = lax.div(local, LANES).astype(F32)
    low = lax.rem(local, LANES).astype(F32)
    held = (lax.broadcasted_iota(jnp.int32, (n, slots), 0) == holder).astype(F32)
    blocks = slots // LANES
    stacked = jnp.concatenate(
        [held[:, b * LANES : (b + 1) * LANES] for b in range(blocks)], axis=0
    ).astype(BF16)
    before = (
        lax.broadcasted_iota(jnp.int32, (LANES, LANES), 0)
        < lax.broadcasted_iota(jnp.int32, (LANES, LANES), 1)
    ).astype(F32)
    counter = jnp.concatenate([before, jnp.ones((LANES, LANES), F32)], axis=1).astype(BF16)
    counts = dot(stacked, counter, NN)
    total = jnp.zeros((n, LANES), F32)
    rank_parts = []
    for b in range(blocks):
        here = counts[b * n : (b + 1) * n]
        place = here[:, :LANES] + total
        rank_parts.append(
            jnp.sum(held[:, b * LANES : (b + 1) * LANES] * place, axis=0, keepdims=True)
        )
        total = total + here[:, LANES:]
    rank = jnp.concatenate(rank_parts, axis=1)
    at_rank = (
        lax.broadcasted_iota(jnp.int32, (LANES, slots), 0).astype(F32) == rank
    ).astype(F32)
    parts = jnp.concatenate([held * high, held * low], axis=0).astype(BF16)
    asked = dot(parts, at_rank.astype(BF16), NT)
    asked = (asked[:n] * float(LANES) + asked[n:]).astype(jnp.int32)
    tall = items.shape[0] // item_rows
    lines = tall - 1
    scale = tall
    send_ids[:, 0, :] = jnp.clip(asked, 0, item_rows - 1) * scale

    for load in loads[:3]:
        load.wait()
    context_part = dot(feature_ref[...], first[:feature_width, :], NN) * 0.5
    send1[0, :, :width] = query_ref[...].astype(F32)
    send1[0, :, width:] = context_part
    for load in loads[3:]:
        load.wait()

    hidden_tiles = hidden_width // LANES
    step = math.gcd(256, item_rows)
    strips = item_rows // step
    early = lax.div(strips * jnp.maximum(groups - 2 * run_me, 0), 2 * groups)

    def project(start, stop):
        @pl.loop(start, stop)
        def visit(i):
            part = pl.ds(pl.multiple_of(i * step, step), step)
            block = table[part]
            projected = dot(block, first[feature_width:, :], NN) * 0.5
            base = pl.multiple_of(i * (step * tall), step * tall)

            def put(j, value):
                items[pl.ds(base + j, step, stride=tall), :] = value

            for j in range(hidden_tiles):
                put(j, projected[:, j * LANES : (j + 1) * LANES])
            for j in range(width // LANES):
                put(hidden_tiles + j, block[:, j * LANES : (j + 1) * LANES].astype(F32))

    project(0, early)
    pl.semaphore_wait(barrier, n - 1)

    def ask(offset):
        if isinstance(offset, int):
            seen = 0
        else:
            plane = lax.rem(run_me + offset, groups)
            seen = turn_at(plane, groups - offset)

        def act(member, peer, where):
            slot = pl.ds(seen * members + member_me, 1)
            pltpu.make_async_remote_copy(
                src_ref=send_ids.at[pl.ds(peer, 1)],
                dst_ref=wanted.at[slot],
                send_sem=send_sem.at[2],
                recv_sem=index_sem.at[seen],
                device_id=where,
                device_id_type=pl.DeviceIdType.MESH,
            ).start()
            pltpu.make_async_remote_copy(
                src_ref=send1,
                dst_ref=recv1.at[slot],
                send_sem=send_sem.at[0],
                recv_sem=arrive_sem.at[seen],
                device_id=where,
                device_id_type=pl.DeviceIdType.MESH,
            ).start()

        each_peer(offset, act)

    def give_back(turn):
        def act(member, peer, where):
            pltpu.make_async_remote_copy(
                src_ref=send2.at[pl.ds(turn * members + member, 1)],
                dst_ref=recv2.at[pl.ds(me, 1)],
                send_sem=send_sem.at[1],
                recv_sem=return_sem,
                device_id=where,
                device_id_type=pl.DeviceIdType.MESH,
            ).start()

        each_peer(offsets[turn], act)

    def wait_ids(group, expected):
        rows = wanted.at[pl.ds(group * members, expected)]
        pltpu.make_async_copy(
            send_ids.at[pl.ds(0, expected)], rows, index_sem.at[group]
        ).wait()

    def wait_rows(buffer, count, semaphore):
        rows = buffer.at[pl.ds(0, count)]
        pltpu.make_async_copy(rows, rows, semaphore).wait()

    for offset in (offsets[1:2] + [0] + offsets[2:]):
        ask(offset)
    own_ids = pltpu.make_async_copy(
        send_ids.at[pl.ds(me, 1)], wanted.at[pl.ds(member_me, 1)], own_sem.at[0]
    )
    own_ids.start()
    own_ask = pltpu.make_async_copy(send1, recv1.at[pl.ds(member_me, 1)], own_sem.at[1])
    own_ask.start()
    second_w[...] = second_w[...] * jnp.asarray(0.5, BF16)
    for b in range(blocks):
        part = slice(b * LANES, (b + 1) * LANES)
        tile_ref[0, b : b + 1] = rank[:, part].astype(jnp.int32)
        tile_ref[1, b : b + 1] = holder[:, part]
    project(early, strips)
    own_ids.wait()
    own_ask.wait()

    lane = lax.broadcasted_iota(jnp.int32, (members, LANES), 1)
    score_row = score_ref[...].reshape(1, hidden_width).astype(F32)
    copies = max(1, LANES // n)
    split = 1 << (math.gcd(4, copies).bit_length() - 1)
    part_rows = item_rows // split

    def gather(turn, batch):
        base = turn * cap * members
        for r in range(cap):
            for b, group in enumerate(batch):
                for c in range(members):
                    at = wanted[group * members + c, 0, r]
                    place = base + (r * len(batch) + b) * members + c
                    found[pl.ds(place * tall, lines)] = items[pl.ds(at, lines)]

    def rank_groups(turn, batch):
        count = cap * members * len(batch)
        base = turn * cap * members

        def found_tile(j):
            return found[pl.ds(base * tall + j, count, stride=tall), :]

        def stacked_rows(low, high):
            return jnp.concatenate(
                [recv1[pl.ds(group * members, members), 0, low:high] for group in batch], axis=0
            )

        query = stacked_rows(0, width)
        context = stacked_rows(width, width + hidden_width)
        item_part = jnp.concatenate([found_tile(j) for j in range(hidden_tiles)], axis=1)
        rows = jnp.concatenate(
            [found_tile(hidden_tiles + j) for j in range(width // LANES)], axis=1
        )
        half = item_part + jnp.concatenate([context] * cap, axis=0)
        hidden = (half + half * jnp.tanh(half)).astype(BF16)
        half = dot(hidden, second_w[...], NN)
        second = (half + half * jnp.tanh(half)).astype(BF16).astype(F32) * score_row
        deep = len(batch) * members
        lanes = lax.broadcasted_iota(jnp.int32, (deep, LANES), 1)
        result = jnp.zeros((deep, LANES), F32)
        for r in range(cap):
            mine = slice(r * deep, (r + 1) * deep)
            score = jnp.sum(second[mine], axis=1, keepdims=True)
            gen = jnp.sum(rows[mine] * query, axis=1, keepdims=True)
            result = jnp.where(lanes == r, score, result)
            result = jnp.where(lanes == gen_at + r, gen, result)
        for b, group in enumerate(batch):
            send2[pl.ds(group * members, members), 0, :] = result[
                b * members : (b + 1) * members
            ]

    def normalizers():
        query = recv1[:, 0, :width]
        blank = jnp.zeros_like(query)
        logits = None
        for part in range(split):
            spread = jnp.concatenate(
                [query if j % split == part else blank for j in range(copies)], axis=0
            ).astype(BF16)
            partial = dot(table[part * part_rows : (part + 1) * part_rows], spread, NT)
            logits = partial if logits is None else logits + partial
        top = jnp.max(logits, axis=0, keepdims=True)
        mass = jnp.sum(jnp.exp(logits - top), axis=0, keepdims=True)
        peak = top
        shifts = [n << k for k in range(split.bit_length() - 1)]
        for shift in shifts:
            peak = jnp.maximum(peak, pltpu.roll(peak, shift, 1))
        mass = mass * jnp.exp(top - peak)
        for shift in shifts:
            mass = mass + pltpu.roll(mass, shift, 1)
        return peak, mass

    def finish(group, peak, mass):
        rows_here = pl.ds(group * members, members)
        across = (members, peak.shape[1])
        mine = lax.broadcasted_iota(jnp.int32, across, 1) == group * members + (
            lax.broadcasted_iota(jnp.int32, across, 0)
        )

        def own_lane(value):
            return jnp.sum(jnp.where(mine, value, 0.0), axis=1, keepdims=True)

        result = jnp.where(lane == max_at, own_lane(peak), send2[rows_here, 0, :])
        send2[rows_here, 0, :] = jnp.where(lane == max_at + 1, own_lane(mass), result)

    once = 1 + lax.div(me, n)

    def arrive(turns):
        @pl.loop(0, once)
        def check(_):
            for turn in turns:
                expected = members if turn else members - 1
                wait_ids(turn, expected)
                wait_rows(recv1, expected, arrive_sem.at[turn])

    arrive([0])
    gather(0, [0])
    rank_groups(0, [0])
    others = list(range(1, groups))
    arrive(others)
    for turn in others[:1]:
        gather(turn, [turn])
    peak, mass = normalizers()
    for turn in others + [0]:
        if turn:
            rank_groups(turn, [turn])
        for later in others[turn : turn + 1] if turn else []:
            gather(later, [later])
        finish(turn, peak, mass)
        give_back(turn)
    own_back = pltpu.make_async_copy(
        send2.at[pl.ds(member_me, 1)], recv2.at[pl.ds(me, 1)], own_sem.at[2]
    )
    own_back.start()
    own_back.wait()
    wait_rows(send_ids, n - 1, send_sem.at[2])
    wait_rows(recv1, n - 1, send_sem.at[0])
    wait_rows(recv2, n - 1, return_sem)

    back = recv2[:, 0, :]
    maxima = back[:, max_at : max_at + 1]
    sums = back[:, max_at + 1 : max_at + 2]
    peak = jnp.max(maxima, axis=0, keepdims=True)
    log_norm = peak + jnp.log(jnp.sum(sums * jnp.exp(maxima - peak), axis=0, keepdims=True))

    rank_tile, holder_tile = tile_ref[0], tile_ref[1]
    gen_tile = rank_tile + gen_at
    tile = (blocks, LANES)

    def look_up(h, found_so_far):
        score, gen = found_so_far
        line = jnp.broadcast_to(recv2[h], tile)
        here = holder_tile == h
        score = jnp.where(here, jnp.take_along_axis(line, rank_tile, axis=1), score)
        gen = jnp.where(here, jnp.take_along_axis(line, gen_tile, axis=1), gen)
        return score, gen

    blank = (jnp.zeros(tile, F32), jnp.zeros(tile, F32))
    if n <= 64:
        score, gen = functools.reduce(lambda value, h: look_up(h, value), range(n), blank)
    else:
        score, gen = lax.fori_loop(0, n, look_up, blank)

    def whole(reduce, value):
        return reduce(reduce(value, axis=0, keepdims=True), axis=1, keepdims=True)

    length = length_ref[0]
    position = lax.broadcasted_iota(jnp.int32, tile, 0) * LANES + lax.broadcasted_iota(
        jnp.int32, tile, 1
    )
    live = position < length
    masked = jnp.where(live, score, -1e30)
    rank_peak = whole(jnp.max, masked)
    rank_norm = rank_peak + jnp.log(
        whole(jnp.sum, jnp.where(live, jnp.exp(masked - rank_peak), 0.0))
    )
    section = jnp.where(
        live, score - rank_norm + gen - log_norm + math.log(item_rows * n), 0.0
    )
    chosen = whole(jnp.sum, jnp.where(position == slot_ref[0], section, 0.0))
    count = jnp.full((1, 1), length, jnp.int32).astype(F32)
    prop = jnp.full((1, 1), prop_ref[0], jnp.int32).astype(F32) / 1024.0
    for b in range(blocks):
        section_ref[:, b * LANES : (b + 1) * LANES] = section[b : b + 1]
    weight_ref[...] = chosen + jnp.log(count) - jnp.log(prop)
    wait_rows(send2, n - 1, send_sem.at[1])


def solution(mesh):
    dp_size, item_size = mesh.shape["dp"], mesh.shape["item"]
    n = dp_size * item_size

    def body(
        query,
        item_table,
        context_features,
        candidates,
        lengths,
        logged_slot,
        logging_prop,
        w_first,
        w_second,
        w_score,
    ):
        slots = candidates.shape[1]
        cap = max(2, 3 * slots // (2 * n))
        width = query.shape[1]
        hidden_width = w_first.shape[1]
        message = width + hidden_width
        tall = round_up((width + hidden_width) // LANES, 8) + 1
        vmem = pl.BlockSpec(memory_space=pltpu.VMEM)
        groups = math.gcd(4, item_size)
        section, weight = pl.pallas_call(
            functools.partial(kernel, dp_size, item_size, groups, cap),
            out_shape=(
                pltpu.VMEM((1, slots), F32),
                pltpu.VMEM((1, 1), F32),
            ),
            in_specs=[pl.BlockSpec(memory_space=pltpu.HBM)] * 10,
            out_specs=(vmem, vmem),
            scratch_shapes=[
                pltpu.VMEM(query.shape, BF16),
                pltpu.VMEM(context_features.shape, BF16),
                pltpu.VMEM(candidates.shape, jnp.int32),
                pltpu.SMEM((1,), jnp.int32),
                pltpu.SMEM((1,), jnp.int32),
                pltpu.SMEM((1,), jnp.int32),
                pltpu.VMEM(w_score.shape, BF16),
                pltpu.VMEM(item_table.shape, BF16),
                pltpu.VMEM(w_first.shape, BF16),
                pltpu.VMEM(w_second.shape, BF16),
                pltpu.VMEM((n, 1, LANES), jnp.int32),
                pltpu.VMEM((1, 1, message), F32),
                pltpu.VMEM((n, 1, message), F32),
                pltpu.VMEM((n, 1, LANES), F32),
                pltpu.VMEM((n, 1, LANES), F32),
                pltpu.SemaphoreType.DMA((10,)),
                pltpu.SemaphoreType.DMA((3,)),
                pltpu.SemaphoreType.DMA((groups,)),
                pltpu.SemaphoreType.DMA((groups,)),
                pltpu.SemaphoreType.DMA,
                pltpu.SemaphoreType.DMA((3,)),
                pltpu.VMEM((item_table.shape[0] * tall, LANES), F32),
                pltpu.VMEM((n * cap * tall + tall, LANES), F32),
                pltpu.SMEM((n, 1, LANES), jnp.int32),
                pltpu.VMEM((2, slots // LANES, LANES), jnp.int32),
            ],
            compiler_params=pltpu.CompilerParams(collective_id=0, has_side_effects=True),
            name="propensity",
        )(
            query,
            context_features,
            candidates,
            lengths,
            logged_slot,
            logging_prop,
            item_table,
            w_first,
            w_second,
            w_score,
        )
        return section, weight.reshape(-1)

    split = P(("dp", "item"))
    rows = P(("dp", "item"), None)
    return jax.shard_map(
        body,
        mesh=mesh,
        in_specs=(rows, rows, rows, rows, split, split, split, P(), P(), P()),
        out_specs=(rows, split),
        check_vma=False,
    )
```

```python
import functools
import math

import jax
import jax.numpy as jnp
from jax import lax
from jax.experimental import pallas as pl
from jax.experimental.pallas import tpu as pltpu
from jax.sharding import PartitionSpec as P

F32 = jnp.float32
BF16 = jnp.bfloat16
LANES = 128
NT = (((1,), (1,)), ((), ()))
NN = (((1,), (0,)), ((), ()))
TN = (((0,), (0,)), ((), ()))


def round_up(value, step):
    return (value + step - 1) // step * step


def dot(left, right, dims):
    return lax.dot_general(left, right, dims, preferred_element_type=F32)


def silu(v):
    half = v * 0.5
    return half + half * jnp.tanh(half)


def kernel(
    dp_size,
    item_size,
    groups,
    cap,
    query_hbm,
    feature_hbm,
    cand_hbm,
    length_hbm,
    slot_hbm,
    prop_hbm,
    table_hbm,
    first_hbm,
    second_hbm,
    score_hbm,
    section_ref,
    query_ref,
    feature_ref,
    cand_ref,
    length_ref,
    slot_ref,
    prop_ref,
    score_ref,
    table,
    first,
    second_w,
    send_ids,
    send1,
    recv1,
    send2,
    recv2,
    load_sem,
    send_sem,
    arrive_sem,
    index_sem,
    return_sem,
    own_sem,
    items,
    found,
    wanted,
    tile_ref,
):
    n = dp_size * item_size
    item_rows, width = table.shape
    slots = cand_ref.shape[1]
    feature_width = feature_ref.shape[1]
    hidden_width = first.shape[1]
    gen_at = round_up(cap, 8)
    max_at = 2 * gen_at
    dp_me, item_me = lax.axis_index("dp"), lax.axis_index("item")
    me = dp_me * item_size + item_me
    run = item_size // groups
    members = dp_size * run
    run_me = lax.div(item_me, run)
    member_me = dp_me * run + lax.rem(item_me, run)

    def device(offset, member):
        dp = lax.div(member, run)
        item = lax.rem(run_me + offset, groups) * run + lax.rem(member, run)
        return dp * item_size + item, {"dp": dp, "item": item}

    def each_peer(offset, act):
        @pl.loop(1 if isinstance(offset, int) else 0, members)
        def visit(j):
            member = lax.rem(member_me + j, members)
            peer, where = device(offset, member)
            act(member, peer, where)

    barrier = pltpu.get_barrier_semaphore()

    def greet(member, peer, where):
        pl.semaphore_signal(barrier, inc=1, device_id=where, device_id_type=pl.DeviceIdType.MESH)

    def farthest(plane):
        end = jnp.where(2 * plane < groups, groups - 1, 0)
        return lax.rem(end - plane + groups, groups)

    def turn_at(plane, offset):
        far = farthest(plane)
        place = offset - 1 - jnp.where(offset > far, 1, 0)
        place = jnp.where(2 * plane < groups, groups - 3 - place, place)
        return jnp.where(offset == far, 1, 2 + place)

    far = farthest(run_me)
    rising = [jnp.where(far <= k, k + 1, k) for k in range(1, groups - 1)]
    middle = [
        jnp.where(2 * run_me < groups, down, up) for up, down in zip(rising, rising[::-1])
    ]
    offsets = [0] + ([far] if groups > 1 else []) + middle
    far_first = offsets[1:] + [0]

    cand_load = pltpu.make_async_copy(cand_hbm, cand_ref, load_sem.at[0])
    cand_load.start()
    for offset in far_first:
        each_peer(offset, greet)

    loads = [
        pltpu.make_async_copy(source, target, load_sem.at[i + 1])
        for i, (source, target) in enumerate(
            [
                (query_hbm, query_ref),
                (feature_hbm, feature_ref),
                (first_hbm, first),
                (table_hbm, table),
                (second_hbm, second_w),
                (score_hbm, score_ref),
                (length_hbm, length_ref),
                (slot_hbm, slot_ref),
                (prop_hbm, prop_ref),
            ]
        )
    ]
    for load in loads:
        load.start()
    cand_load.wait()

    ids = cand_ref[...]
    holder = lax.div(ids, item_rows)
    local = ids - holder * item_rows
    high = lax.div(local, LANES).astype(F32)
    low = lax.rem(local, LANES).astype(F32)
    held = (lax.broadcasted_iota(jnp.int32, (n, slots), 0) == holder).astype(F32)
    blocks = slots // LANES
    stacked = jnp.concatenate(
        [held[:, b * LANES : (b + 1) * LANES] for b in range(blocks)], axis=0
    ).astype(BF16)
    before = (
        lax.broadcasted_iota(jnp.int32, (LANES, LANES), 0)
        < lax.broadcasted_iota(jnp.int32, (LANES, LANES), 1)
    ).astype(F32)
    counter = jnp.concatenate([before, jnp.ones((LANES, LANES), F32)], axis=1).astype(BF16)
    counts = dot(stacked, counter, NN)
    total = jnp.zeros((n, LANES), F32)
    rank_parts = []
    for b in range(blocks):
        here = counts[b * n : (b + 1) * n]
        place = here[:, :LANES] + total
        rank_parts.append(
            jnp.sum(held[:, b * LANES : (b + 1) * LANES] * place, axis=0, keepdims=True)
        )
        total = total + here[:, LANES:]
    rank = jnp.concatenate(rank_parts, axis=1)
    at_rank = (
        lax.broadcasted_iota(jnp.int32, (LANES, slots), 0).astype(F32) == rank
    ).astype(F32)
    parts = jnp.concatenate([held * high, held * low], axis=0).astype(BF16)
    asked = dot(parts, at_rank.astype(BF16), NT)
    asked = (asked[:n] * float(LANES) + asked[n:]).astype(jnp.int32)
    tall = items.shape[0] // item_rows
    lines = tall - 1
    scale = tall
    send_ids[:, 0, :] = jnp.clip(asked, 0, item_rows - 1) * scale

    for load in loads[:3]:
        load.wait()
    context_part = dot(feature_ref[...], first[:feature_width, :], NN) * 0.5
    send1[0, :, :width] = query_ref[...].astype(F32)
    send1[0, :, width:] = context_part
    for load in loads[3:]:
        load.wait()

    hidden_tiles = hidden_width // LANES
    step = math.gcd(256, item_rows)
    strips = item_rows // step
    early = lax.div(strips * jnp.maximum(groups - 2 * run_me, 0), 2 * groups)

    def project(start, stop):
        @pl.loop(start, stop)
        def visit(i):
            part = pl.ds(pl.multiple_of(i * step, step), step)
            block = table[part]
            projected = dot(block, first[feature_width:, :], NN) * 0.5
            base = pl.multiple_of(i * (step * tall), step * tall)

            def put(j, value):
                items[pl.ds(base + j, step, stride=tall), :] = value

            for j in range(hidden_tiles):
                put(j, projected[:, j * LANES : (j + 1) * LANES])
            for j in range(width // LANES):
                put(hidden_tiles + j, block[:, j * LANES : (j + 1) * LANES].astype(F32))

    project(0, early)
    pl.semaphore_wait(barrier, n - 1)

    def ask(offset):
        if isinstance(offset, int):
            seen = 0
        else:
            plane = lax.rem(run_me + offset, groups)
            seen = turn_at(plane, groups - offset)

        def act(member, peer, where):
            slot = pl.ds(seen * members + member_me, 1)
            pltpu.make_async_remote_copy(
                src_ref=send_ids.at[pl.ds(peer, 1)],
                dst_ref=wanted.at[slot],
                send_sem=send_sem.at[2],
                recv_sem=index_sem.at[seen],
                device_id=where,
                device_id_type=pl.DeviceIdType.MESH,
            ).start()
            pltpu.make_async_remote_copy(
                src_ref=send1,
                dst_ref=recv1.at[slot],
                send_sem=send_sem.at[0],
                recv_sem=arrive_sem.at[seen],
                device_id=where,
                device_id_type=pl.DeviceIdType.MESH,
            ).start()

        each_peer(offset, act)

    def give_back(turn):
        def act(member, peer, where):
            pltpu.make_async_remote_copy(
                src_ref=send2.at[pl.ds(turn * members + member, 1)],
                dst_ref=recv2.at[pl.ds(me, 1)],
                send_sem=send_sem.at[1],
                recv_sem=return_sem,
                device_id=where,
                device_id_type=pl.DeviceIdType.MESH,
            ).start()

        each_peer(offsets[turn], act)

    def wait_ids(group, expected):
        rows = wanted.at[pl.ds(group * members, expected)]
        pltpu.make_async_copy(
            send_ids.at[pl.ds(0, expected)], rows, index_sem.at[group]
        ).wait()

    def wait_rows(buffer, count, semaphore):
        rows = buffer.at[pl.ds(0, count)]
        pltpu.make_async_copy(rows, rows, semaphore).wait()

    for offset in (offsets[1:2] + [0] + offsets[2:]):
        ask(offset)
    own_ids = pltpu.make_async_copy(
        send_ids.at[pl.ds(me, 1)], wanted.at[pl.ds(member_me, 1)], own_sem.at[0]
    )
    own_ids.start()
    own_ask = pltpu.make_async_copy(send1, recv1.at[pl.ds(member_me, 1)], own_sem.at[1])
    own_ask.start()
    second_w[...] = second_w[...] * jnp.asarray(0.5, BF16)
    for b in range(blocks):
        part = slice(b * LANES, (b + 1) * LANES)
        tile_ref[0, b : b + 1] = rank[:, part].astype(jnp.int32)
        tile_ref[1, b : b + 1] = holder[:, part]
    project(early, strips)
    own_ids.wait()
    own_ask.wait()

    lane = lax.broadcasted_iota(jnp.int32, (members, LANES), 1)
    score_row = score_ref[...].reshape(1, hidden_width).astype(F32)
    copies = max(1, LANES // n)
    split = 1 << (math.gcd(4, copies).bit_length() - 1)
    part_rows = item_rows // split

    def gather(turn, batch):
        base = turn * cap * members
        for r in range(cap):
            for b, group in enumerate(batch):
                for c in range(members):
                    at = wanted[group * members + c, 0, r]
                    place = base + (r * len(batch) + b) * members + c
                    found[pl.ds(place * tall, lines)] = items[pl.ds(at, lines)]

    def rank_groups(turn, batch):
        count = cap * members * len(batch)
        base = turn * cap * members

        def found_tile(j):
            return found[pl.ds(base * tall + j, count, stride=tall), :]

        def stacked_rows(low, high):
            return jnp.concatenate(
                [recv1[pl.ds(group * members, members), 0, low:high] for group in batch], axis=0
            )

        query = stacked_rows(0, width)
        context = stacked_rows(width, width + hidden_width)
        item_part = jnp.concatenate([found_tile(j) for j in range(hidden_tiles)], axis=1)
        rows = jnp.concatenate(
            [found_tile(hidden_tiles + j) for j in range(width // LANES)], axis=1
        )
        half = item_part + jnp.concatenate([context] * cap, axis=0)
        hidden = (half + half * jnp.tanh(half)).astype(BF16)
        half = dot(hidden, second_w[...], NN)
        second = (half + half * jnp.tanh(half)).astype(BF16).astype(F32) * score_row
        deep = len(batch) * members
        lanes = lax.broadcasted_iota(jnp.int32, (deep, LANES), 1)
        result = jnp.zeros((deep, LANES), F32)
        for r in range(cap):
            mine = slice(r * deep, (r + 1) * deep)
            score = jnp.sum(second[mine], axis=1, keepdims=True)
            gen = jnp.sum(rows[mine] * query, axis=1, keepdims=True)
            result = jnp.where(lanes == r, score, result)
            result = jnp.where(lanes == gen_at + r, gen, result)
        for b, group in enumerate(batch):
            send2[pl.ds(group * members, members), 0, :] = result[
                b * members : (b + 1) * members
            ]

    def normalizers():
        query = recv1[:, 0, :width]
        blank = jnp.zeros_like(query)
        logits = None
        for part in range(split):
            spread = jnp.concatenate(
                [query if j % split == part else blank for j in range(copies)], axis=0
            ).astype(BF16)
            partial = dot(table[part * part_rows : (part + 1) * part_rows], spread, NT)
            logits = partial if logits is None else logits + partial
        top = jnp.max(logits, axis=0, keepdims=True)
        mass = jnp.sum(jnp.exp(logits - top), axis=0, keepdims=True)
        peak = top
        shifts = [n << k for k in range(split.bit_length() - 1)]
        for shift in shifts:
            peak = jnp.maximum(peak, pltpu.roll(peak, shift, 1))
        mass = mass * jnp.exp(top - peak)
        for shift in shifts:
            mass = mass + pltpu.roll(mass, shift, 1)
        return peak, mass

    def finish(group, peak, mass):
        rows_here = pl.ds(group * members, members)
        across = (members, peak.shape[1])
        mine = lax.broadcasted_iota(jnp.int32, across, 1) == group * members + (
            lax.broadcasted_iota(jnp.int32, across, 0)
        )

        def own_lane(value):
            return jnp.sum(jnp.where(mine, value, 0.0), axis=1, keepdims=True)

        result = jnp.where(lane == max_at, own_lane(peak), send2[rows_here, 0, :])
        send2[rows_here, 0, :] = jnp.where(lane == max_at + 1, own_lane(mass), result)

    once = 1 + lax.div(me, n)

    def arrive(turns):
        @pl.loop(0, once)
        def check(_):
            for turn in turns:
                expected = members if turn else members - 1
                wait_ids(turn, expected)
                wait_rows(recv1, expected, arrive_sem.at[turn])

    arrive([0])
    gather(0, [0])
    rank_groups(0, [0])
    others = list(range(1, groups))
    arrive(others)
    for turn in others[:1]:
        gather(turn, [turn])
    peak, mass = normalizers()
    for turn in others + [0]:
        if turn:
            rank_groups(turn, [turn])
        for later in others[turn : turn + 1] if turn else []:
            gather(later, [later])
        finish(turn, peak, mass)
        give_back(turn)
    own_back = pltpu.make_async_copy(
        send2.at[pl.ds(member_me, 1)], recv2.at[pl.ds(me, 1)], own_sem.at[2]
    )
    own_back.start()
    own_back.wait()
    wait_rows(send_ids, n - 1, send_sem.at[2])
    wait_rows(recv1, n - 1, send_sem.at[0])
    wait_rows(recv2, n - 1, return_sem)

    back = recv2[:, 0, :]
    maxima = back[:, max_at : max_at + 1]
    sums = back[:, max_at + 1 : max_at + 2]
    peak = jnp.max(maxima, axis=0, keepdims=True)
    log_norm = peak + jnp.log(jnp.sum(sums * jnp.exp(maxima - peak), axis=0, keepdims=True))

    rank_tile, holder_tile = tile_ref[0], tile_ref[1]
    gen_tile = rank_tile + gen_at
    tile = (blocks, LANES)

    def look_up(h, found_so_far):
        score, gen = found_so_far
        line = jnp.broadcast_to(recv2[h], tile)
        here = holder_tile == h
        score = jnp.where(here, jnp.take_along_axis(line, rank_tile, axis=1), score)
        gen = jnp.where(here, jnp.take_along_axis(line, gen_tile, axis=1), gen)
        return score, gen

    blank = (jnp.zeros(tile, F32), jnp.zeros(tile, F32))
    if n <= 64:
        score, gen = functools.reduce(lambda value, h: look_up(h, value), range(n), blank)
    else:
        score, gen = lax.fori_loop(0, n, look_up, blank)

    def whole(reduce, value):
        return reduce(reduce(value, axis=0, keepdims=True), axis=1, keepdims=True)

    length = length_ref[0]
    position = lax.broadcasted_iota(jnp.int32, tile, 0) * LANES + lax.broadcasted_iota(
        jnp.int32, tile, 1
    )
    live = position < length
    masked = jnp.where(live, score, -1e30)
    rank_peak = whole(jnp.max, masked)
    rank_norm = rank_peak + jnp.log(
        whole(jnp.sum, jnp.where(live, jnp.exp(masked - rank_peak), 0.0))
    )
    section = jnp.where(
        live, score - rank_norm + gen - log_norm + math.log(item_rows * n), 0.0
    )
    chosen = whole(jnp.sum, jnp.where(position == slot_ref[0], section, 0.0))
    count = jnp.full((1, 1), length, jnp.int32).astype(F32)
    prop = jnp.full((1, 1), prop_ref[0], jnp.int32).astype(F32) / 1024.0
    for b in range(blocks):
        section_ref[:, b * LANES : (b + 1) * LANES] = section[b : b + 1]
    section_ref[:, slots:] = jnp.broadcast_to(
        chosen + jnp.log(count) - jnp.log(prop), (1, LANES)
    )
    wait_rows(send2, n - 1, send_sem.at[1])


def solution(mesh):
    dp_size, item_size = mesh.shape["dp"], mesh.shape["item"]
    n = dp_size * item_size

    def body(
        query,
        item_table,
        context_features,
        candidates,
        lengths,
        logged_slot,
        logging_prop,
        w_first,
        w_second,
        w_score,
    ):
        slots = candidates.shape[1]
        cap = max(2, 3 * slots // (2 * n))
        width = query.shape[1]
        hidden_width = w_first.shape[1]
        message = width + hidden_width
        tall = round_up((width + hidden_width) // LANES, 8) + 1
        vmem = pl.BlockSpec(memory_space=pltpu.VMEM)
        groups = math.gcd(4, item_size)
        (packed,) = pl.pallas_call(
            functools.partial(kernel, dp_size, item_size, groups, cap),
            out_shape=(
                pltpu.VMEM((1, slots + LANES), F32),
            ),
            in_specs=[pl.BlockSpec(memory_space=pltpu.HBM)] * 10,
            out_specs=(vmem,),
            scratch_shapes=[
                pltpu.VMEM(query.shape, BF16),
                pltpu.VMEM(context_features.shape, BF16),
                pltpu.VMEM(candidates.shape, jnp.int32),
                pltpu.SMEM((1,), jnp.int32),
                pltpu.SMEM((1,), jnp.int32),
                pltpu.SMEM((1,), jnp.int32),
                pltpu.VMEM(w_score.shape, BF16),
                pltpu.VMEM(item_table.shape, BF16),
                pltpu.VMEM(w_first.shape, BF16),
                pltpu.VMEM(w_second.shape, BF16),
                pltpu.VMEM((n, 1, LANES), jnp.int32),
                pltpu.VMEM((1, 1, message), F32),
                pltpu.VMEM((n, 1, message), F32),
                pltpu.VMEM((n, 1, LANES), F32),
                pltpu.VMEM((n, 1, LANES), F32),
                pltpu.SemaphoreType.DMA((10,)),
                pltpu.SemaphoreType.DMA((3,)),
                pltpu.SemaphoreType.DMA((groups,)),
                pltpu.SemaphoreType.DMA((groups,)),
                pltpu.SemaphoreType.DMA,
                pltpu.SemaphoreType.DMA((3,)),
                pltpu.VMEM((item_table.shape[0] * tall, LANES), F32),
                pltpu.VMEM((n * cap * tall + tall, LANES), F32),
                pltpu.SMEM((n, 1, LANES), jnp.int32),
                pltpu.VMEM((2, slots // LANES, LANES), jnp.int32),
            ],
            compiler_params=pltpu.CompilerParams(collective_id=0, has_side_effects=True),
            name="propensity",
        )(
            query,
            context_features,
            candidates,
            lengths,
            logged_slot,
            logging_prop,
            item_table,
            w_first,
            w_second,
            w_score,
        )
        return packed[:, :slots], packed[0, slots : slots + 1]

    split = P(("dp", "item"))
    rows = P(("dp", "item"), None)
    return jax.shard_map(
        body,
        mesh=mesh,
        in_specs=(rows, rows, rows, rows, split, split, split, P(), P(), P()),
        out_specs=(rows, split),
        check_vma=False,
    )
```
